512 devices in a mesh: prow: 32 (over y_lo, z), pcol: 16 (over y_hi, x, core).
Axes of the slice: x: 4, y: 4 (y_hi: 2, y_lo: 2; y = y_hi * 2 + y_lo), z: 16, core: 2. Of those that a mesh axis runs over, the one named last changes fastest.
Arguments:
- slab: bfloat16 [16384, 4096], P('prow', 'pcol'), may hold values from -6 to 6
- panels: bfloat16 [1, 16384, 512], P(None, 'prow', 'pcol'), may hold values from -0.25 to 0.25
- pivots: int32 [1, 512], replicated, may hold values from 0 to 16383, as said below
Outputs:
- factored_slab: bfloat16 [16384, 4096], P('prow', 'pcol')
The draws below stay inside these ranges and needn't reach their ends.
Inputs may be any that keep to these rules, and one draw needn't show every extreme that they name: pivots[j, k] lies between j * 512 + k and 16383.
All inputs are finite; a program needn't handle non-finite values.
Results may differ from the reference program's by a relative error of at most 0.0041.
Values may be sent and summed in bfloat16 or wider, within the bound.
A program may use at most 64 MiB of HBM per device.

```python
import jax
import jax.numpy as jnp
from jax import lax

BLOCK_COLS = 512
PANELS = 1
COLS_DEV = 256
ROWS = 16384
COLS = 4096
N_PCOL = 16


def draw_pivots(key, part):
    starts = (jnp.arange(PANELS, dtype=jnp.int32)[:, None] * BLOCK_COLS + jnp.arange(BLOCK_COLS, dtype=jnp.int32)[None, :]).astype(jnp.int32)
    picks = jax.random.randint(key, (PANELS, BLOCK_COLS), starts, ROWS, dtype=jnp.int32)
    picks = picks.at[0, 0].set(0)
    picks = picks.at[PANELS - 1, BLOCK_COLS - 1].set(ROWS - 1)
    return picks


def steps_of(key, extent, cuts, least, largest):
    level, own = 1.0, jax.random.fold_in(key, 6)
    for position, parts in cuts:
        heights = jnp.exp(jax.random.uniform(jax.random.fold_in(own, position), (parts,), jnp.float32, least / len(cuts), largest / len(cuts)))
        level = level * jnp.repeat(heights, extent[position] // parts).reshape([-1 if axis == position else 1 for axis in range(len(extent))])
    return level


def centred(key, dims, deviation, reach, pieces=(), kind=jnp.bfloat16):
    gain = steps_of(key, dims, pieces, -0.22, 0.18) if pieces else 1.0
    entries = jax.random.normal(key, dims, jnp.float32) * deviation * gain
    return jnp.minimum(jnp.maximum(entries, -reach), reach).astype(kind)


def setup_inputs(seed: int = 0) -> dict:
    splits = jax.random.split(jax.random.key(seed), 4)
    slab = centred(splits[0], (ROWS, COLS), 1.0, 6.0, ((0, 32), (1, 16)))
    panels = centred(splits[1], (PANELS, ROWS, BLOCK_COLS), BLOCK_COLS ** -0.5, 0.25, ((1, 32), (2, 16)))
    pivots = draw_pivots(jax.random.fold_in(splits[3], 71), 0)
    return dict(slab=slab, panels=panels, pivots=pivots)


def interchange(pivot_row, top_row, total_rows):

    def apply_swap(index, order):
        target = top_row + index
        source = pivot_row[index]
        first_value = order[target]
        second_value = order[source]
        return order.at[target].set(second_value).at[source].set(first_value)
    return lax.fori_loop(0, pivot_row.shape[0], apply_swap, jnp.arange(total_rows, dtype=jnp.int32))

def one_block(column_block, panels, orders):
    current = column_block
    for panel_index in range(PANELS):
        top_row = panel_index * BLOCK_COLS
        current = jnp.take(current, orders[panel_index], axis=0)
        top_block = current[top_row:top_row + BLOCK_COLS].astype(jnp.float32)
        diagonal = panels[panel_index, top_row:top_row + BLOCK_COLS].astype(jnp.float32)
        upper_rows = jax.scipy.linalg.solve_triangular(diagonal, top_block, lower=True, unit_diagonal=True).astype(jnp.bfloat16)
        below = panels[panel_index, top_row + BLOCK_COLS:]
        product = jnp.dot(below.astype(jnp.float32), upper_rows.astype(jnp.float32), preferred_element_type=jnp.float32)
        updated = (current[top_row + BLOCK_COLS:].astype(jnp.float32) - product).astype(jnp.bfloat16)
        current = jnp.concatenate([current[:top_row], upper_rows, updated], axis=0)
    return current

def reference(slab, panels, pivots):
    orders = jnp.stack([interchange(pivots[panel_index], panel_index * BLOCK_COLS, ROWS) for panel_index in range(PANELS)], axis=0)
    blocks = jnp.transpose(slab.reshape(ROWS, N_PCOL, COLS_DEV), (1, 0, 2))
    results = lax.map(lambda column_block: one_block(column_block, panels, orders), blocks)
    return jnp.transpose(results, (1, 0, 2)).reshape(ROWS, COLS)
```

```python
import jax
import jax.numpy as jnp
from jax import lax
from jax.experimental import pallas as pl
from jax.experimental.pallas import tpu as pltpu
from jax.sharding import PartitionSpec as P

BLOCK = 512
CAP = 32
NZ = 16
MESH = pl.DeviceIdType.MESH
F32 = jnp.float32
BF16 = jnp.bfloat16
I32 = jnp.int32


def general(slab, panels, pivots):
    def gathered(x, axis):
        n = lax.axis_size(axis)
        return lax.all_to_all(jnp.broadcast_to(x[None], (n, *x.shape)), axis, 0, 0, tiled=True)

    rows_local, cols_local = slab.shape
    row_start = lax.axis_index("prow") * rows_local
    global_rows = row_start + jnp.arange(rows_local, dtype=I32)
    steps = jnp.arange(BLOCK, dtype=I32)
    pivot_row = pivots[0]
    earlier = steps[:, None] < steps[None, :]
    hit = (pivot_row[:, None] == steps[None, :]) & earlier
    parent = jnp.max(jnp.where(hit, steps[:, None], -1), axis=0)
    pointer = jnp.where(parent >= 0, parent, steps)
    pointer = lax.fori_loop(0, 10, lambda _, p: jnp.take(p, p), pointer)
    same = (pivot_row[:, None] == pivot_row[None, :]) & earlier
    latest = jnp.max(jnp.where(same, steps[:, None], -1), axis=0)
    top_source = jnp.where(latest >= 0, jnp.take(pointer, jnp.clip(latest, 0, BLOCK - 1)), pivot_row)
    local_source = top_source - row_start
    is_mine = (local_source >= 0) & (local_source < rows_local)
    fetched = jnp.take(slab, jnp.clip(local_source, 0, rows_local - 1), axis=0)
    picked = jnp.where(is_mine[:, None], fetched, jnp.zeros_like(fetched))
    top = gathered(picked, "prow").astype(F32).sum(axis=0)
    old_top = gathered(slab, "prow")[0]
    diagonal = gathered(gathered(panels[0], "prow")[0], "pcol")
    diagonal = jnp.moveaxis(diagonal, 0, 1).reshape(BLOCK, BLOCK).astype(F32)
    upper = jax.scipy.linalg.solve_triangular(diagonal, top, lower=True, unit_diagonal=True).astype(BF16)
    match = global_rows[:, None] == pivot_row[None, :]
    last_hit = jnp.max(jnp.where(match, steps[None, :], -1), axis=1)
    displaced = (last_hit >= 0) & (global_rows >= BLOCK)
    moved = jnp.take(old_top, jnp.take(pointer, jnp.clip(last_hit, 0, BLOCK - 1)), axis=0)
    swapped = jnp.where(displaced[:, None], moved, slab)
    whole = jnp.moveaxis(gathered(panels[0], "pcol"), 0, 1).reshape(rows_local, BLOCK)
    product = jnp.dot(whole, upper, preferred_element_type=F32)
    updated = (swapped.astype(F32) - product).astype(BF16)
    return jnp.where(row_start == 0, upper, updated)


def iota(shape, dim):
    return lax.broadcasted_iota(I32, shape, dim)


def ones(mask):
    return jnp.where(mask, 1.0, 0.0).astype(BF16)


def dot(a, b):
    return jnp.dot(a, b, preferred_element_type=F32)


def dot_nt(a, b):
    return lax.dot_general(a, b, (((1,), (1,)), ((), ())), preferred_element_type=F32)


def dot_f32(a, b):
    return jnp.dot(a, b, preferred_element_type=F32, precision=lax.Precision.HIGHEST)


def column(row):
    n = row.shape[1]
    blocks = [jnp.broadcast_to(row[:, i : i + 128], (128, 128)).astype(F32).T[:, :1] for i in range(0, n, 128)]
    return jnp.concatenate(blocks, axis=0).astype(I32)


def lower_inverse(block):
    i, j = iota((128, 128), 0), iota((128, 128), 1)
    eye = jnp.where(i == j, 1.0, 0.0)
    inv = []
    for d in range(4):
        full = block(d, d)
        n = jnp.where((i // 16 == j // 16) & (i > j), full, 0.0)
        m, p = eye - n, n
        for _ in range(3):
            p = dot_f32(p, p)
            m = m + dot_f32(m, p)
        for size in (16, 32, 64):
            b = jnp.where((i // (2 * size) == j // (2 * size)) & (i // size > j // size), full, 0.0)
            m = m - dot_f32(m, dot_f32(b, m))
        inv.append(m)
    lower = {}
    for d in (0, 2):
        lower[d] = -dot_f32(inv[d + 1], dot_f32(block(d + 1, d), inv[d]))
    zero = jnp.zeros((128, 128), F32)
    first = jnp.concatenate([jnp.concatenate([inv[0], zero], 1), jnp.concatenate([lower[0], inv[1]], 1)], 0)
    second = jnp.concatenate([jnp.concatenate([inv[2], zero], 1), jnp.concatenate([lower[2], inv[3]], 1)], 0)
    corner = jnp.concatenate(
        [jnp.concatenate([block(2, 0), block(2, 1)], 1), jnp.concatenate([block(3, 0), block(3, 1)], 1)], 0
    )
    third = -dot_f32(second, dot_f32(corner, first))
    zero = jnp.zeros((256, 256), F32)
    return jnp.concatenate([jnp.concatenate([first, zero], 1), jnp.concatenate([third, second], 1)], 0)


def kernel(
    slab, panel, pivot, out, over,
    cand, pbuf, lbuf, zbuf, zsend,
    c_send, c_recv, p_send, p_recv, l_send, l_recv, lz_send, z_send, z_recv, ready,
):
    r, c = lax.axis_index("prow"), lax.axis_index("pcol")
    y, z = r // NZ, r % NZ

    def at(dz):
        return (y * NZ + (z + dz + NZ) % NZ, c)

    partner = ((1 - y) * NZ + z, c)
    root = (0, c)

    def peer(i):
        return (r, (c + i) % 16)

    def copy(src, dst, send, recv, device):
        return pltpu.make_async_remote_copy(
            src_ref=src, dst_ref=dst, send_sem=send, recv_sem=recv, device_id=device, device_id_type=MESH
        )

    near = (1, -1, 2, -2, 3, -3, 4, -4)
    barrier = pltpu.get_barrier_semaphore()

    def hello(device):
        pl.semaphore_signal(barrier, inc=1, device_id=device, device_id_type=MESH)

    for dz in near:
        hello(at(dz))
    hello(partner)
    for i in range(1, 16):
        hello(peer(i))
    far_from_root = (y == 0) & (z > 4) & (z < 12)

    @pl.when(r == 0)
    def _():
        for dz in range(5, 12):
            hello((dz, c))

    p_row = pivot[...]
    b_row = p_row // BLOCK
    k_row = iota((1, BLOCK), 1)
    before = iota((BLOCK, BLOCK), 0) < iota((BLOCK, BLOCK), 1)
    in_block = iota((32, BLOCK), 0) == b_row
    counts = dot(ones(in_block), ones(before))
    rank_row = jnp.sum(jnp.where(in_block, counts, 0.0), axis=0, keepdims=True).astype(I32)
    p_col = column(p_row)
    equal = p_col == p_row
    later_row = jnp.max(jnp.where(equal & (iota((BLOCK, BLOCK), 0) > iota((BLOCK, BLOCK), 1)), 1, 0), axis=0, keepdims=True)
    hit_row = jnp.max(jnp.where(p_col == iota((BLOCK, BLOCK), 1), 1, 0), axis=0, keepdims=True)
    goes_on = ones((p_row < BLOCK) | (later_row > 0))
    next_goes_on = dot(goes_on, ones(iota((BLOCK, BLOCK), 0) == p_row))
    stays_row = ones((hit_row > 0) | (later_row > 0) | (next_goes_on > 0))
    rank0_row = dot(stays_row, ones(before)).astype(I32)
    far_row = p_row >= BLOCK
    slots = iota((CAP, BLOCK), 0)
    mine = jnp.where((b_row == r) & far_row, 1, 0) * jnp.where(rank_row == slots, 1, 0)
    local_hit = ones(iota((BLOCK, BLOCK), 0) + r * BLOCK == p_row)
    pack = dot_nt(ones(mine > 0), local_hit)
    pack0 = jnp.where((rank0_row == slots) & (stays_row > 0), 1.0, 0.0)
    pack = jnp.where(r == 0, pack0, pack).astype(BF16)
    cand[r] = dot(pack, slab[...]).astype(BF16)
    full = jnp.max(jnp.where(far_row, rank_row, 0), axis=1, keepdims=True)
    full0 = jnp.max(jnp.where(stays_row > 0, rank0_row, 0), axis=1, keepdims=True)
    over[0, 0] = jnp.max(jnp.maximum(full, full0))
    pbuf[c] = panel[...]

    pl.semaphore_wait(barrier, 24 + jnp.where(far_from_root, 1, 0))

    sends, c_wait = [], {}

    def send_cand(n, slot, device):
        t = copy(cand.at[slot], cand.at[slot], c_send.at[n], c_recv.at[slot], device)
        t.start()
        sends.append(t)

    def wait_cand(slot):
        copy(cand.at[slot], cand.at[slot], c_send.at[0], c_recv.at[slot], partner).wait_recv()

    def slot_of(dz):
        return y * NZ + (z + dz + NZ) % NZ

    for n, dz in enumerate((4, -4, 3, -3, 2, -2, 1, -1)):
        send_cand(n, r, at(dz))
    send_cand(8, r, partner)

    @pl.when((y == 0) & (z > 0))
    def _():
        pl.semaphore_signal(ready.at[z], inc=1, device_id=root, device_id_type=MESH)

    for i in range(1, 16):
        copy(panel, pbuf.at[c], p_send.at[i], p_recv.at[c], peer(i)).start()

    @pl.when(r == 0)
    def _():
        for dz in (1, 2, 3, 4, 15, 14, 13, 12, 5, 6, 7, 11, 10, 9, 8):
            pl.semaphore_wait(ready.at[dz], 1)
            copy(panel, lbuf.at[c], lz_send.at[dz], l_recv.at[c], (dz, c)).start()
        copy(panel, lbuf.at[c], lz_send.at[0], l_recv.at[c], partner).start()

    kk = iota((BLOCK, BLOCK), 0)
    jj = iota((BLOCK, BLOCK), 1)
    parent = jnp.max(jnp.where((p_row == kk) & (jj < kk), jj, -1), axis=1, keepdims=True)
    k_col = iota((BLOCK, 1), 0)
    chain = ones(jnp.where(parent >= 0, parent, k_col) == jj)

    def square(times, a):
        for _ in range(times):
            a = dot(a, a).astype(BF16)
        return a

    chain = square(4, chain)

    n = 9
    for dz in (4, 3, 2, 1):
        wait_cand(slot_of(dz))
        send_cand(n, slot_of(dz), at(-4))
        n += 1
        wait_cand(slot_of(-dz))
        if dz < 4:
            send_cand(n, slot_of(-dz), at(4))
            n += 1
    for dz in (4, -4, 3, -3, 2, -2, 1, -1):
        send_cand(n, slot_of(dz), partner)
        n += 1

    chain = square(5, chain)
    slot_row = jnp.where(far_row, b_row * CAP + rank_row, -1)

    @pl.when(r == 0)
    def _():
        content = dot(chain, slab[...]).astype(BF16)
        for q in range(0, 32, 4):
            pick = ones(slot_row == iota((4 * CAP, BLOCK), 0) + q * CAP)
            zsend[q : q + 4] = dot(pick, content).astype(BF16).reshape(4, CAP, 256)

    latest = jnp.max(jnp.where(equal & (jj < kk), jj, -1), axis=1, keepdims=True)
    source = dot(ones(latest == jj), chain) + jnp.where((latest < 0) & (p_col == jj), 1.0, 0.0)
    rank0_col = column(jnp.where(stays_row > 0, rank0_row, -1))
    near_pick = dot(source.astype(BF16), ones(rank0_col == iota((BLOCK, CAP), 1)))
    slot_col = column(slot_row)
    far_pick = ones((slot_col == iota((BLOCK, 32 * CAP), 1)) & (latest < 0))
    pick = jnp.concatenate([near_pick.astype(BF16), far_pick[:, CAP:]], axis=1)

    for dz in (5, 6, 7, 8, -5, -6, -7):
        wait_cand(slot_of(dz))
        send_cand(n, slot_of(dz), partner)
        n += 1

    @pl.when(r == 0)
    def _():
        for dz in range(1, NZ):
            copy(zsend.at[dz], zbuf.at[0], z_send.at[dz], z_recv.at[0], (dz, c)).start()
            copy(zsend.at[NZ + dz], zbuf.at[1], z_send.at[NZ + dz], z_recv.at[1], (dz, c)).start()
        copy(zsend.at[NZ], zbuf.at[0], z_send.at[NZ], z_recv.at[0], partner).start()

    def wait_shard(buf, sem, i):
        copy(buf.at[i], buf.at[i], p_send.at[1], sem.at[i], partner).wait_recv()

    @pl.when(r > 0)
    def _():
        wait_shard(lbuf, l_recv, c)

        @pl.when(y == 0)
        def _():
            copy(lbuf.at[c], lbuf.at[c], l_send.at[0], l_recv.at[c], partner).start()

        for i in range(1, 16):
            copy(lbuf.at[c], lbuf.at[c], l_send.at[i], l_recv.at[c], peer(i)).start()

    for i in range(1, 16):
        wait_shard(pbuf, p_recv, (c + i) % 16)

    @pl.when(r == 0)
    def _():
        lbuf[...] = pbuf[...]

    @pl.when(r > 0)
    def _():
        for i in range(1, 16):
            wait_shard(lbuf, l_recv, (c + i) % 16)

    panel_t = pbuf[...].reshape(BLOCK, BLOCK)
    diagonal_t = lbuf[...].reshape(BLOCK, BLOCK)

    def block(a, b):
        return diagonal_t[128 * b : 128 * b + 128, 128 * a : 128 * a + 128].astype(F32).T

    inverse = lower_inverse(block)
    high = inverse.astype(BF16)
    low = (inverse - high.astype(F32)).astype(BF16)

    for dz in range(NZ):
        wait_cand((1 - y) * NZ + dz)
    top = dot(pick, cand[...].reshape(32 * CAP, 256)).astype(BF16)
    upper = (dot(high, top) + dot(low, top)).astype(BF16)

    @pl.when(r > 0)
    def _():
        copy(zbuf.at[0], zbuf.at[0], z_send.at[0], z_recv.at[0], partner).wait_recv()

        @pl.when((y == 0) & (z > 0))
        def _():
            copy(zbuf.at[1], zbuf.at[1], z_send.at[0], z_recv.at[1], partner).wait_recv()
            copy(zbuf.at[1], zbuf.at[0], z_send.at[0], z_recv.at[0], partner).start()

        last = jnp.where(later_row > 0, 0, mine)
        place = dot_nt(local_hit, ones(last > 0))
        moved = dot(place.astype(BF16), zbuf[0])
        hit = jnp.sum(place, axis=1, keepdims=True) > 0
        product = lax.dot_general(panel_t, upper, (((0,), (0,)), ((), ())), preferred_element_type=F32)
        out[...] = (jnp.where(hit, moved, slab[...].astype(F32)) - product).astype(BF16)

    @pl.when(r == 0)
    def _():
        out[...] = upper

    for t in sends:
        t.wait_send()
    for i in range(1, 16):
        copy(panel, pbuf.at[c], p_send.at[i], p_recv.at[c], peer(i)).wait_send()

    @pl.when(r > 0)
    def _():
        for i in range(1, 16):
            copy(lbuf.at[c], lbuf.at[c], l_send.at[i], l_recv.at[c], peer(i)).wait_send()

        @pl.when(y == 0)
        def _():
            copy(lbuf.at[c], lbuf.at[c], l_send.at[0], l_recv.at[c], partner).wait_send()
            copy(zbuf.at[1], zbuf.at[0], z_send.at[0], z_recv.at[0], partner).wait_send()

    @pl.when(r == 0)
    def _():
        for dz in range(NZ):
            copy(panel, lbuf.at[c], lz_send.at[dz], l_recv.at[c], partner).wait_send()
        for dz in range(1, 32):
            copy(zsend.at[dz], zbuf.at[0], z_send.at[dz], z_recv.at[0], partner).wait_send()


def local(slab, panels, pivots):
    vmem = pl.BlockSpec(memory_space=pltpu.VMEM)
    dma = pltpu.SemaphoreType.DMA
    out, over = pl.pallas_call(
        kernel,
        out_shape=(jax.ShapeDtypeStruct(slab.shape, BF16), jax.ShapeDtypeStruct((1, 1), I32)),
        in_specs=[vmem] * 3,
        out_specs=(vmem, pl.BlockSpec(memory_space=pltpu.SMEM)),
        scratch_shapes=[
            pltpu.VMEM((32, CAP, 256), BF16),
            pltpu.VMEM((16, 32, BLOCK), BF16),
            pltpu.VMEM((16, 32, BLOCK), BF16),
            pltpu.VMEM((2, CAP, 256), BF16),
            pltpu.VMEM((32, CAP, 256), BF16),
            dma((32,)), dma((32,)), dma((16,)), dma((16,)), dma((16,)), dma((16,)), dma((16,)), dma((32,)), dma((2,)),
            pltpu.SemaphoreType.REGULAR((16,)),
        ],
        compiler_params=pltpu.CompilerParams(collective_id=0, has_side_effects=True),
        name="lu_update",
    )(slab, jnp.transpose(panels[0]), pivots)
    return lax.cond(over[0, 0] >= CAP, general, lambda *_: out, slab, panels, pivots)


def solution(mesh):
    in_specs = (P("prow", "pcol"), P(None, "prow", "pcol"), P())
    out_specs = P("prow", "pcol")
    return jax.shard_map(local, mesh=mesh, in_specs=in_specs, out_specs=out_specs, check_vma=False)
```

```python
import jax
import jax.numpy as jnp
from jax import lax
from jax.experimental import pallas as pl
from jax.experimental.pallas import tpu as pltpu
from jax.sharding import PartitionSpec as P

BLOCK = 512
CAP = 32
NZ = 16
MESH = pl.DeviceIdType.MESH
F32 = jnp.float32
BF16 = jnp.bfloat16
I32 = jnp.int32


def general(slab, panels, pivots):
    def gathered(x, axis):
        n = lax.axis_size(axis)
        return lax.all_to_all(jnp.broadcast_to(x[None], (n, *x.shape)), axis, 0, 0, tiled=True)

    rows_local, cols_local = slab.shape
    row_start = lax.axis_index("prow") * rows_local
    global_rows = row_start + jnp.arange(rows_local, dtype=I32)
    steps = jnp.arange(BLOCK, dtype=I32)
    pivot_row = pivots[0]
    earlier = steps[:, None] < steps[None, :]
    hit = (pivot_row[:, None] == steps[None, :]) & earlier
    parent = jnp.max(jnp.where(hit, steps[:, None], -1), axis=0)
    pointer = jnp.where(parent >= 0, parent, steps)
    pointer = lax.fori_loop(0, 10, lambda _, p: jnp.take(p, p), pointer)
    same = (pivot_row[:, None] == pivot_row[None, :]) & earlier
    latest = jnp.max(jnp.where(same, steps[:, None], -1), axis=0)
    top_source = jnp.where(latest >= 0, jnp.take(pointer, jnp.clip(latest, 0, BLOCK - 1)), pivot_row)
    local_source = top_source - row_start
    is_mine = (local_source >= 0) & (local_source < rows_local)
    fetched = jnp.take(slab, jnp.clip(local_source, 0, rows_local - 1), axis=0)
    picked = jnp.where(is_mine[:, None], fetched, jnp.zeros_like(fetched))
    top = gathered(picked, "prow").astype(F32).sum(axis=0)
    old_top = gathered(slab, "prow")[0]
    diagonal = gathered(gathered(panels[0], "prow")[0], "pcol")
    diagonal = jnp.moveaxis(diagonal, 0, 1).reshape(BLOCK, BLOCK).astype(F32)
    upper = jax.scipy.linalg.solve_triangular(diagonal, top, lower=True, unit_diagonal=True).astype(BF16)
    match = global_rows[:, None] == pivot_row[None, :]
    last_hit = jnp.max(jnp.where(match, steps[None, :], -1), axis=1)
    displaced = (last_hit >= 0) & (global_rows >= BLOCK)
    moved = jnp.take(old_top, jnp.take(pointer, jnp.clip(last_hit, 0, BLOCK - 1)), axis=0)
    swapped = jnp.where(displaced[:, None], moved, slab)
    whole = jnp.moveaxis(gathered(panels[0], "pcol"), 0, 1).reshape(rows_local, BLOCK)
    product = jnp.dot(whole, upper, preferred_element_type=F32)
    updated = (swapped.astype(F32) - product).astype(BF16)
    return jnp.where(row_start == 0, upper, updated)


def iota(shape, dim):
    return lax.broadcasted_iota(I32, shape, dim)


def ones(mask):
    return jnp.where(mask, 1.0, 0.0).astype(BF16)


def dot(a, b):
    return jnp.dot(a, b, preferred_element_type=F32)


def dot_nt(a, b):
    return lax.dot_general(a, b, (((1,), (1,)), ((), ())), preferred_element_type=F32)


def column(row):
    n = row.shape[1]
    blocks = [jnp.broadcast_to(row[:, i : i + 128], (128, 128)).astype(F32).T[:, :1] for i in range(0, n, 128)]
    return jnp.concatenate(blocks, axis=0).astype(I32)


def split(x):
    high = x.astype(BF16)
    return high, (x - high.astype(F32)).astype(BF16)


def dot_f32(a, b):
    a_parts = (a,) if a.dtype == BF16 else split(a)
    b_parts = (b,) if b.dtype == BF16 else split(b)
    total = dot(a_parts[0], b_parts[0])
    if len(b_parts) > 1:
        total += dot(a_parts[0], b_parts[1])
    if len(a_parts) > 1:
        total += dot(a_parts[1], b_parts[0])
    return total


def lower_inverse(block):
    i, j = iota((128, 128), 0), iota((128, 128), 1)
    eye = jnp.where(i == j, 1.0, 0.0)
    inv, full, power = [], [], []
    for d in range(4):
        full.append(block(d, d))
        n = jnp.where((i // 16 == j // 16) & (i > j), full[d].astype(F32), 0.0)
        inv.append(eye - n)
        power.append(n.astype(BF16))
    for _ in range(3):
        for d in range(4):
            power[d] = dot_f32(power[d], power[d])
        for d in range(4):
            inv[d] = inv[d] + dot_f32(inv[d], power[d])
    for size in (16, 32, 64):
        off = (i // (2 * size) == j // (2 * size)) & (i // size > j // size)
        step = [dot_f32(jnp.where(off, full[d].astype(F32), 0.0).astype(BF16), inv[d]) for d in range(4)]
        for d in range(4):
            inv[d] = inv[d] - dot_f32(inv[d], step[d])
    zero = jnp.zeros((128, 128), F32)
    halves = []
    for d in (0, 2):
        lower = -dot_f32(inv[d + 1], dot_f32(block(d + 1, d), inv[d]))
        halves.append(jnp.concatenate([jnp.concatenate([inv[d], zero], 1), jnp.concatenate([lower, inv[d + 1]], 1)], 0))
    return halves


def kernel(
    slab, panel, pivot, out, over,
    cand, pbuf, lbuf, zbuf, zsend, straight,
    c_send, c_recv, p_send, p_recv, l_send, l_recv, lz_send, z_send, z_recv, ready,
):
    r, c = lax.axis_index("prow"), lax.axis_index("pcol")
    y, z = r // NZ, r % NZ

    def ring(dz):
        return (z + dz + NZ) % NZ

    def at(dz):
        return (y * NZ + ring(dz), c)

    partner = ((1 - y) * NZ + z, c)

    def peer(i):
        return (r, (c + i) % 16)

    def copy(src, dst, send, recv, device):
        return pltpu.make_async_remote_copy(
            src_ref=src, dst_ref=dst, send_sem=send, recv_sem=recv, device_id=device, device_id_type=MESH
        )

    near = (4, -4, 3, -3, 2, -2, 1, -1)
    barrier = pltpu.get_barrier_semaphore()

    def hello(device):
        pl.semaphore_signal(barrier, inc=1, device_id=device, device_id_type=MESH)

    hello(partner)
    for i in range(1, 16):
        hello(peer(i))
    for dz in near:

        @pl.when(ring(dz) > z)
        def _(dz=dz):
            hello(at(dz))

    @pl.when(z == 0)
    def _():
        for dz in range(5, 12):
            hello(at(dz))

    p_row = pivot[...]
    b_row = p_row // BLOCK
    before = iota((BLOCK, BLOCK), 0) < iota((BLOCK, BLOCK), 1)
    in_block = iota((32, BLOCK), 0) == b_row
    counts = dot(ones(in_block), ones(before))
    rank_row = jnp.sum(jnp.where(in_block, counts, 0.0), axis=0, keepdims=True).astype(I32)
    p_col = column(p_row)
    equal = p_col == p_row
    later_row = jnp.max(jnp.where(equal & (iota((BLOCK, BLOCK), 0) > iota((BLOCK, BLOCK), 1)), 1, 0), axis=0, keepdims=True)
    hit_row = jnp.max(jnp.where(p_col == iota((BLOCK, BLOCK), 1), 1, 0), axis=0, keepdims=True)
    goes_on = ones((p_row < BLOCK) | (later_row > 0))
    next_goes_on = dot(goes_on, ones(iota((BLOCK, BLOCK), 0) == p_row))
    stays_row = ones((hit_row > 0) | (later_row > 0) | (next_goes_on > 0))
    rank0_row = dot(stays_row, ones(before)).astype(I32)
    far_row = p_row >= BLOCK
    slots = iota((CAP, BLOCK), 0)
    mine = jnp.where((b_row == r) & far_row, 1, 0) * jnp.where(rank_row == slots, 1, 0)
    local_hit = ones(iota((BLOCK, BLOCK), 0) + r * BLOCK == p_row)
    pack = dot_nt(ones(mine > 0), local_hit)
    pack0 = jnp.where((rank0_row == slots) & (stays_row > 0), 1.0, 0.0)
    pack = jnp.where(r == 0, pack0, pack).astype(BF16)
    cand[r] = dot(pack, slab[...]).astype(BF16)
    pbuf[c] = panel[...]

    @pl.when(r == 0)
    def _():
        lbuf[c] = panel[...]

    pl.semaphore_wait(
        barrier, 16 + jnp.minimum(z, 4) + jnp.maximum(z - 11, 0) + jnp.where((z > 4) & (z < 12), 1, 0)
    )

    def announce(device):
        pl.semaphore_signal(ready.at[z], inc=1, device_id=device, device_id_type=MESH)

    @pl.when((z > 4) & (z < 12))
    def _():
        announce((y * NZ, c))

    for dz in near:

        @pl.when(ring(dz) < z)
        def _(dz=dz):
            announce(at(dz))

    def send_cand(n, slot, device):
        t = copy(cand.at[slot], cand.at[slot], c_send.at[n], c_recv.at[slot], device)
        t.start()

    def wait_cand(slot):
        copy(cand.at[slot], cand.at[slot], c_send.at[0], c_recv.at[slot], partner).wait_recv()

    def slot_of(dz):
        return y * NZ + ring(dz)

    def send_shard(n, device):
        copy(lbuf.at[c], lbuf.at[c], lz_send.at[n], l_recv.at[c], device).start()

    def wait_shard(buf, sem, i):
        copy(buf.at[i], buf.at[i], p_send.at[1], sem.at[i], partner).wait_recv()

    @pl.when(r == 0)
    def _():
        send_shard(0, partner)

    for n, dz in enumerate(near):

        @pl.when(ring(dz) < z)
        def _(n=n, dz=dz):
            send_cand(n, r, at(dz))

    send_cand(8, r, partner)
    for i in range(1, 16):
        copy(panel, pbuf.at[c], p_send.at[i], p_recv.at[c], peer(i)).start()

    def spread_shard():
        for i in range(1, 16):
            copy(lbuf.at[c], lbuf.at[c], l_send.at[i], l_recv.at[c], peer(i)).start()

    @pl.when((r > 0) & (z < 5))
    def _():
        wait_shard(lbuf, l_recv, c)
        spread_shard()

    def root_sends(steps):
        @pl.when(z == 0)
        def _():
            for dz in steps:
                pl.semaphore_wait(ready.at[dz], 1)
                send_shard(dz, at(dz))
                if dz < 5 or dz > 11:
                    send_cand(near.index(dz if dz < 5 else dz - NZ), r, at(dz))

    root_sends((1, 2, 3, 4))

    kk = iota((BLOCK, BLOCK), 0)
    jj = iota((BLOCK, BLOCK), 1)
    parent = jnp.max(jnp.where((p_row == kk) & (jj < kk), jj, -1), axis=1, keepdims=True)
    k_col = iota((BLOCK, 1), 0)
    chain = ones(jnp.where(parent >= 0, parent, k_col) == jj)

    def square(times, a):
        for _ in range(times):
            a = dot(a, a).astype(BF16)
        return a

    for n, dz in enumerate(near):

        @pl.when((z > 0) & (ring(dz) > z))
        def _(n=n, dz=dz):
            pl.semaphore_wait(ready.at[ring(dz)], 1)
            send_cand(n, r, at(dz))

    chain = square(4, chain)
    root_sends((5, 15, 14, 13, 12, 6, 7, 11, 10, 9, 8))

    n = 9
    for dz in (4, 3, 2, 1):
        wait_cand(slot_of(dz))
        send_cand(n, slot_of(dz), at(-4))
        n += 1
        wait_cand(slot_of(-dz))
        if dz < 4:
            send_cand(n, slot_of(-dz), at(4))
            n += 1
    for dz in near:
        send_cand(n, slot_of(dz), partner)
        n += 1

    @pl.when(z > 4)
    def _():
        wait_shard(lbuf, l_recv, c)
        spread_shard()

    chain = square(5, chain)
    slot_row = jnp.where(far_row, b_row * CAP + rank_row, -1)

    @pl.when(r == 0)
    def _():
        content = dot(chain, slab[...]).astype(BF16)
        for q in range(0, 32, 4):
            pick = ones(slot_row == iota((4 * CAP, BLOCK), 0) + q * CAP)
            zsend[q : q + 4] = dot(pick, content).astype(BF16).reshape(4, CAP, 256)

    full = jnp.max(jnp.where(far_row, rank_row, 0), axis=1, keepdims=True)
    full0 = jnp.max(jnp.where(stays_row > 0, rank0_row, 0), axis=1, keepdims=True)
    over[0, 0] = jnp.max(jnp.maximum(full, full0))
    latest = jnp.max(jnp.where(equal & (jj < kk), jj, -1), axis=1, keepdims=True)
    source = dot(ones(latest == jj), chain) + jnp.where((latest < 0) & (p_col == jj), 1.0, 0.0)
    rank0_col = column(jnp.where(stays_row > 0, rank0_row, -1))
    near_pick = dot(source.astype(BF16), ones(rank0_col == iota((BLOCK, CAP), 1)))
    slot_col = column(slot_row)
    far_pick = ones((slot_col == iota((BLOCK, 32 * CAP), 1)) & (latest < 0))
    pick = jnp.concatenate([near_pick.astype(BF16), far_pick[:, CAP:]], axis=1)

    def other_ring():
        half = zsend.at[pl.ds(NZ, NZ)]
        return copy(half, half, z_send.at[0], z_recv.at[1], partner)

    @pl.when(r == 0)
    def _():
        other_ring().start()

    @pl.when(r == NZ)
    def _():
        other_ring().wait_recv()
        zbuf[...] = zsend[NZ]

    @pl.when(z == 0)
    def _():
        for dz in range(1, NZ):
            copy(zsend.at[y * NZ + dz], zbuf, z_send.at[dz], z_recv.at[0], at(dz)).start()

    for dz in (5, 6, 7, 8, -5, -6, -7):
        wait_cand(slot_of(dz))
        send_cand(n, slot_of(dz), partner)
        n += 1

    for i in range(1, 16):
        wait_shard(pbuf, p_recv, (c + i) % 16)

    @pl.when(r == 0)
    def _():
        for i in range(1, 16):
            lbuf[(c + i) % 16] = pbuf[(c + i) % 16]

    panel_t = pbuf[...].reshape(BLOCK, BLOCK)
    for a in range(0, BLOCK, 128):
        for b in range(0, BLOCK, 128):
            straight[b : b + 128, a : a + 128] = panel_t[a : a + 128, b : b + 128].astype(F32).T.astype(BF16)

    @pl.when(r > 0)
    def _():
        for i in range(1, 16):
            wait_shard(lbuf, l_recv, (c + i) % 16)

    diagonal_t = lbuf[...].reshape(BLOCK, BLOCK)

    def block(a, b):
        return diagonal_t[128 * b : 128 * b + 128, 128 * a : 128 * a + 128].astype(F32).T.astype(BF16)

    first, second = lower_inverse(block)
    corner = jnp.concatenate(
        [jnp.concatenate([block(2, 0), block(2, 1)], 1), jnp.concatenate([block(3, 0), block(3, 1)], 1)], 0
    )
    first_high, first_low = split(first)
    second_high, second_low = split(second)

    for dz in range(NZ):
        wait_cand((1 - y) * NZ + dz)
    top = dot(pick, cand[...].reshape(32 * CAP, 256))
    half = top[:256].astype(BF16)
    upper1 = dot(first_high, half) + dot(first_low, half)
    high1, low1 = split(upper1)
    high2, low2 = split(top[256:] - (dot(corner, high1) + dot(corner, low1)))
    upper2 = dot(second_high, high2) + dot(second_high, low2) + dot(second_low, high2)
    upper = jnp.concatenate([high1, upper2.astype(BF16)], axis=0)

    @pl.when(r > 0)
    def _():
        @pl.when(z > 0)
        def _():
            copy(zbuf, zbuf, z_send.at[0], z_recv.at[0], partner).wait_recv()

        last = jnp.where(later_row > 0, 0, mine)
        place = dot_nt(local_hit, ones(last > 0))
        moved = dot(place.astype(BF16), zbuf[...])
        hit = jnp.sum(place, axis=1, keepdims=True) > 0
        product = dot(straight[...], upper)
        out[...] = (jnp.where(hit, moved, slab[...].astype(F32)) - product).astype(BF16)

    @pl.when(r == 0)
    def _():
        out[...] = upper

    for i in range(31):
        copy(cand.at[r], cand.at[r], c_send.at[i], c_recv.at[r], partner).wait_send()
    for i in range(1, 16):
        copy(panel, pbuf.at[c], p_send.at[i], p_recv.at[c], peer(i)).wait_send()

    @pl.when(r > 0)
    def _():
        for i in range(1, 16):
            copy(lbuf.at[c], lbuf.at[c], l_send.at[i], l_recv.at[c], peer(i)).wait_send()

    @pl.when(z == 0)
    def _():
        for dz in range(1, NZ):
            copy(lbuf.at[c], lbuf.at[c], lz_send.at[dz], l_recv.at[c], partner).wait_send()
            copy(zsend.at[dz], zbuf, z_send.at[dz], z_recv.at[0], partner).wait_send()

    @pl.when(r == 0)
    def _():
        copy(lbuf.at[c], lbuf.at[c], lz_send.at[0], l_recv.at[c], partner).wait_send()
        other_ring().wait_send()


def local(slab, panels, pivots):
    vmem = pl.BlockSpec(memory_space=pltpu.VMEM)
    dma = pltpu.SemaphoreType.DMA
    out, over = pl.pallas_call(
        kernel,
        out_shape=(jax.ShapeDtypeStruct(slab.shape, BF16), jax.ShapeDtypeStruct((1, 1), I32)),
        in_specs=[vmem] * 3,
        out_specs=(vmem, pl.BlockSpec(memory_space=pltpu.SMEM)),
        scratch_shapes=[
            pltpu.VMEM((32, CAP, 256), BF16),
            pltpu.VMEM((16, 32, BLOCK), BF16),
            pltpu.VMEM((16, 32, BLOCK), BF16),
            pltpu.VMEM((CAP, 256), BF16),
            pltpu.VMEM((32, CAP, 256), BF16),
            pltpu.VMEM((BLOCK, BLOCK), BF16),
            dma((32,)), dma((32,)), dma((16,)), dma((16,)), dma((16,)), dma((16,)), dma((16,)), dma((16,)), dma((2,)),
            pltpu.SemaphoreType.REGULAR((16,)),
        ],
        compiler_params=pltpu.CompilerParams(collective_id=0, has_side_effects=True),
        name="lu_update",
    )(slab, jnp.transpose(panels[0]), pivots)
    return lax.cond(over[0, 0] >= CAP, general, lambda *_: out, slab, panels, pivots)


def solution(mesh):
    in_specs = (P("prow", "pcol"), P(None, "prow", "pcol"), P())
    out_specs = P("prow", "pcol")
    return jax.shard_map(local, mesh=mesh, in_specs=in_specs, out_specs=out_specs, check_vma=False)
```

```python
import jax
import jax.numpy as jnp
from jax import lax
from jax.experimental import pallas as pl
from jax.experimental.pallas import tpu as pltpu
from jax.sharding import PartitionSpec as P

BLOCK = 512
CAP = 32
NZ = 16
MESH = pl.DeviceIdType.MESH
F32 = jnp.float32
BF16 = jnp.bfloat16
I32 = jnp.int32


def general(slab, panels, pivots):
    def gathered(x, axis):
        n = lax.axis_size(axis)
        return lax.all_to_all(jnp.broadcast_to(x[None], (n, *x.shape)), axis, 0, 0, tiled=True)

    rows_local, cols_local = slab.shape
    row_start = lax.axis_index("prow") * rows_local
    global_rows = row_start + jnp.arange(rows_local, dtype=I32)
    steps = jnp.arange(BLOCK, dtype=I32)
    pivot_row = pivots[0]
    earlier = steps[:, None] < steps[None, :]
    hit = (pivot_row[:, None] == steps[None, :]) & earlier
    parent = jnp.max(jnp.where(hit, steps[:, None], -1), axis=0)
    pointer = jnp.where(parent >= 0, parent, steps)
    pointer = lax.fori_loop(0, 10, lambda _, p: jnp.take(p, p), pointer)
    same = (pivot_row[:, None] == pivot_row[None, :]) & earlier
    latest = jnp.max(jnp.where(same, steps[:, None], -1), axis=0)
    top_source = jnp.where(latest >= 0, jnp.take(pointer, jnp.clip(latest, 0, BLOCK - 1)), pivot_row)
    local_source = top_source - row_start
    is_mine = (local_source >= 0) & (local_source < rows_local)
    fetched = jnp.take(slab, jnp.clip(local_source, 0, rows_local - 1), axis=0)
    picked = jnp.where(is_mine[:, None], fetched, jnp.zeros_like(fetched))
    top = gathered(picked, "prow").astype(F32).sum(axis=0)
    old_top = gathered(slab, "prow")[0]
    diagonal = gathered(gathered(panels[0], "prow")[0], "pcol")
    diagonal = jnp.moveaxis(diagonal, 0, 1).reshape(BLOCK, BLOCK).astype(F32)
    upper = jax.scipy.linalg.solve_triangular(diagonal, top, lower=True, unit_diagonal=True).astype(BF16)
    match = global_rows[:, None] == pivot_row[None, :]
    last_hit = jnp.max(jnp.where(match, steps[None, :], -1), axis=1)
    displaced = (last_hit >= 0) & (global_rows >= BLOCK)
    moved = jnp.take(old_top, jnp.take(pointer, jnp.clip(last_hit, 0, BLOCK - 1)), axis=0)
    swapped = jnp.where(displaced[:, None], moved, slab)
    whole = jnp.moveaxis(gathered(panels[0], "pcol"), 0, 1).reshape(rows_local, BLOCK)
    product = jnp.dot(whole, upper, preferred_element_type=F32)
    updated = (swapped.astype(F32) - product).astype(BF16)
    return jnp.where(row_start == 0, upper, updated)


def iota(shape, dim):
    return lax.broadcasted_iota(I32, shape, dim)


def ones(mask):
    return jnp.where(mask, 1.0, 0.0).astype(BF16)


def dot(a, b):
    return jnp.dot(a, b, preferred_element_type=F32)


def dot_nt(a, b):
    return lax.dot_general(a, b, (((1,), (1,)), ((), ())), preferred_element_type=F32)


def column(row):
    n = row.shape[1]
    blocks = [jnp.broadcast_to(row[:, i : i + 128], (128, 128)).astype(F32).T[:, :1] for i in range(0, n, 128)]
    return jnp.concatenate(blocks, axis=0).astype(I32)


def split(x):
    high = x.astype(BF16)
    return high, (x - high.astype(F32)).astype(BF16)


def dot_f32(a, b):
    a_parts = (a,) if a.dtype == BF16 else split(a)
    b_parts = (b,) if b.dtype == BF16 else split(b)
    total = dot(a_parts[0], b_parts[0])
    if len(b_parts) > 1:
        total += dot(a_parts[0], b_parts[1])
    if len(a_parts) > 1:
        total += dot(a_parts[1], b_parts[0])
    return total


def lower_inverse(block):
    i, j = iota((128, 128), 0), iota((128, 128), 1)
    eye = jnp.where(i == j, 1.0, 0.0)
    inv, full, power = [], [], []
    for d in range(4):
        full.append(block(d, d))
        n = jnp.where((i // 16 == j // 16) & (i > j), full[d].astype(F32), 0.0)
        inv.append(eye - n)
        power.append(n.astype(BF16))
    for _ in range(3):
        for d in range(4):
            power[d] = dot_f32(power[d], power[d])
        for d in range(4):
            inv[d] = inv[d] + dot_f32(inv[d], power[d])
    for size in (16, 32, 64):
        off = (i // (2 * size) == j // (2 * size)) & (i // size > j // size)
        step = [dot_f32(jnp.where(off, full[d].astype(F32), 0.0).astype(BF16), inv[d]) for d in range(4)]
        for d in range(4):
            inv[d] = inv[d] - dot_f32(inv[d], step[d])
    zero = jnp.zeros((128, 128), F32)
    halves = []
    for d in (0, 2):
        lower = -dot_f32(inv[d + 1], dot_f32(block(d + 1, d), inv[d]))
        halves.append(jnp.concatenate([jnp.concatenate([inv[d], zero], 1), jnp.concatenate([lower, inv[d + 1]], 1)], 0))
    return halves


def kernel(
    slab, panel, pivot, out, over,
    cand, pbuf, lbuf, zbuf, zsend, straight,
    c_send, c_recv, p_send, p_recv, l_send, l_recv, lz_send, z_send, z_recv, ready,
):
    r, c = lax.axis_index("prow"), lax.axis_index("pcol")
    y, z = r // NZ, r % NZ

    def ring(dz):
        return (z + dz + NZ) % NZ

    def at(dz):
        return (y * NZ + ring(dz), c)

    partner = ((1 - y) * NZ + z, c)

    across = (c + 8) % 16

    def peer(i):
        return (r, (c // 8) * 8 + (c + i) % 8) if i < 8 else (r, across)

    def copy(src, dst, send, recv, device):
        return pltpu.make_async_remote_copy(
            src_ref=src, dst_ref=dst, send_sem=send, recv_sem=recv, device_id=device, device_id_type=MESH
        )

    near = (4, -4, 3, -3, 2, -2, 1, -1)
    barrier = pltpu.get_barrier_semaphore()

    def hello(device):
        pl.semaphore_signal(barrier, inc=1, device_id=device, device_id_type=MESH)

    hello(partner)
    for i in range(1, 9):
        hello(peer(i))
    for dz in near:

        @pl.when(ring(dz) > z)
        def _(dz=dz):
            hello(at(dz))

    @pl.when(z == 0)
    def _():
        for dz in range(5, 12):
            hello(at(dz))

    pl.semaphore_wait(
        barrier, 9 + jnp.minimum(z, 4) + jnp.maximum(z - 11, 0) + jnp.where((z > 4) & (z < 12), 1, 0)
    )

    def announce(device):
        pl.semaphore_signal(ready.at[z], inc=1, device_id=device, device_id_type=MESH)

    @pl.when((z > 4) & (z < 12))
    def _():
        announce((y * NZ, c))

    for dz in near:

        @pl.when(ring(dz) < z)
        def _(dz=dz):
            announce(at(dz))

    def send_cand(slot, device, recv=None):
        copy(cand.at[slot], cand.at[slot], c_send.at[0], c_recv.at[slot if recv is None else recv], device).start()

    def wait_cand(slot):
        copy(cand.at[slot], cand.at[slot], c_send.at[0], c_recv.at[slot], partner).wait_recv()

    def slot_of(dz):
        return y * NZ + ring(dz)

    def send_shard(n, device):
        copy(lbuf.at[c], lbuf.at[c], lz_send.at[n], l_recv.at[2], device).start()

    def wait_shards(buf, sem, count):
        some = buf.at[pl.ds(0, count)]
        copy(some, some, p_send.at[0], sem, partner).wait_recv()

    @pl.when(r == 0)
    def _():
        copy(panel, lbuf.at[c], lz_send.at[0], l_recv.at[2], partner).start()
        lbuf[c] = panel[...]

    p_row = pivot[...]
    b_row = p_row // BLOCK
    far_row = p_row >= BLOCK
    before = ones(iota((BLOCK, BLOCK), 0) < iota((BLOCK, BLOCK), 1))
    in_block = iota((32, BLOCK), 0) == b_row
    counts = dot(ones(in_block), before)
    rank_row = jnp.sum(jnp.where(in_block, counts, 0.0), axis=0, keepdims=True).astype(I32)
    slots = iota((CAP, BLOCK), 0)
    mine = jnp.where((b_row == r) & far_row, 1, 0) * jnp.where(rank_row == slots, 1, 0)
    local_hit = ones(iota((BLOCK, BLOCK), 0) + r * BLOCK == p_row)

    def top_slots():
        p_col = column(p_row)
        later = (p_col == p_row) & (iota((BLOCK, BLOCK), 0) > iota((BLOCK, BLOCK), 1))
        later_row = jnp.max(jnp.where(later, 1, 0), axis=0, keepdims=True)
        hit_row = jnp.max(jnp.where(p_col == iota((BLOCK, BLOCK), 1), 1, 0), axis=0, keepdims=True)
        goes_on = ones((p_row < BLOCK) | (later_row > 0))
        next_goes_on = dot(goes_on, ones(iota((BLOCK, BLOCK), 0) == p_row))
        stays_row = ones((hit_row > 0) | (later_row > 0) | (next_goes_on > 0))
        return p_col, later_row, stays_row, dot(stays_row, before).astype(I32)

    slot_row = jnp.where(far_row, b_row * CAP + rank_row, -1)

    def chain_roots():
        k, j = iota((BLOCK, BLOCK), 0), iota((BLOCK, BLOCK), 1)
        parent = jnp.max(jnp.where((p_row == k) & (j < k), j, -1), axis=1, keepdims=True)
        a = ones(jnp.where(parent >= 0, parent, iota((BLOCK, 1), 0)) == j)
        return lax.fori_loop(0, 9, lambda _, a: dot(a, a).astype(BF16), a)

    @pl.when(r > 0)
    def _():
        pack = dot_nt(ones(mine > 0), local_hit)
        cand[r] = dot(pack.astype(BF16), slab[...]).astype(BF16)

    @pl.when(r == 0)
    def _():
        _, _, stays, rank0 = top_slots()
        cand[r] = dot(ones((rank0 == slots) & (stays > 0)), slab[...]).astype(BF16)

    for dz in near:

        @pl.when(ring(dz) < z)
        def _(dz=dz):
            send_cand(r, at(dz))

    send_cand(r, partner, y * NZ)

    def root_sends(steps, shard, slot):
        @pl.when(z == 0)
        def _():
            for dz in steps:
                if slot is not None:
                    pl.semaphore_wait(ready.at[dz], 1)
                if slot:
                    send_cand(r, at(dz))
                if shard:
                    send_shard(dz, at(dz))

    @pl.when(r == NZ)
    def _():
        wait_shards(lbuf, l_recv.at[2], 1)

    root_sends((1, 2, 3, 4), True, True)
    root_sends((15, 14, 13, 12), False, True)
    root_sends((5, 6, 7), True, False)
    root_sends((11, 10, 9, 8), True, False)
    root_sends((12, 13, 14, 15), True, None)

    @pl.when(z > 4)
    def _():
        for dz in near:

            @pl.when(ring(dz) > z)
            def _(dz=dz):
                pl.semaphore_wait(ready.at[ring(dz)], 1)
                send_cand(r, at(dz))

    def spread(src, buf, send, recv):
        for i in range(8, 0, -1):
            copy(src, buf.at[c], send.at[0], recv.at[1 if i == 8 else 0], peer(i)).start()

    def spread_on(buf, send, recv):
        wait_shards(buf, recv.at[1], 1)
        for i in range(1, 8):
            copy(buf.at[across], buf.at[across], send.at[0], recv.at[0], peer(i)).start()

    def spread_done(buf, send, recv):
        some = buf.at[pl.ds(0, 15)]
        copy(some, some, send.at[0], recv.at[0], partner).wait_send()

    pbuf[c] = panel[...]
    spread(panel, pbuf, p_send, p_recv)

    def spread_shard():
        spread(lbuf.at[c], lbuf, l_send, l_recv)

    @pl.when(r == NZ)
    def _():
        spread_shard()

    @pl.when((z > 0) & (z < 5))
    def _():
        for dz in (1, 2, 3, 4, -1, -2, -3, -4):

            @pl.when(ring(dz) > z)
            def _(dz=dz):
                pl.semaphore_wait(ready.at[ring(dz)], 1)
                send_cand(r, at(dz))

        wait_shards(lbuf, l_recv.at[2], 1)
        spread_shard()

    @pl.when(r == 0)
    def _():
        content = dot(chain_roots(), slab[...]).astype(BF16)
        for q in range(0, 32, 4):
            pick = ones(slot_row == iota((4 * CAP, BLOCK), 0) + q * CAP)
            zsend[q % NZ : q % NZ + 4, q // NZ] = dot(pick, content).astype(BF16).reshape(4, CAP, 256)

    p_col, later_row, stays_row, rank0_row = top_slots()
    kk = iota((BLOCK, BLOCK), 0)
    jj = iota((BLOCK, BLOCK), 1)

    for dz in (4, 3, 2, 1):
        wait_cand(slot_of(dz))
        send_cand(slot_of(dz), at(-4))
        wait_cand(slot_of(-dz))
        if dz < 4:
            send_cand(slot_of(-dz), at(4))
    for dz in near:
        send_cand(slot_of(dz), partner, y * NZ)

    spread_on(pbuf, p_send, p_recv)

    def pass_on(rows):
        return copy(rows, zbuf.at[0], z_send.at[0], z_recv.at[0], partner)

    @pl.when(r == 0)
    def _():
        for dz in range(1, NZ):
            copy(zsend.at[dz], zbuf, z_send.at[dz], z_recv.at[0], at(dz)).start()
        pass_on(zsend.at[0, 1]).start()

    @pl.when(z > 4)
    def _():
        wait_shards(lbuf, l_recv.at[2], 1)
        spread_shard()

    chain = chain_roots()
    full = jnp.max(jnp.where(far_row, rank_row, 0), axis=1, keepdims=True)
    full0 = jnp.max(jnp.where(stays_row > 0, rank0_row, 0), axis=1, keepdims=True)
    over[0, 0] = jnp.max(jnp.maximum(full, full0))
    latest = jnp.max(jnp.where((p_col == p_row) & (jj < kk), jj, -1), axis=1, keepdims=True)
    source = dot(ones(latest == jj), chain) + jnp.where((latest < 0) & (p_col == jj), 1.0, 0.0)
    rank0_col = column(jnp.where(stays_row > 0, rank0_row, -1))
    near_pick = dot(source.astype(BF16), ones(rank0_col == iota((BLOCK, CAP), 1)))
    slot_col = column(slot_row)
    far_pick = ones((slot_col == iota((BLOCK, 32 * CAP), 1)) & (latest < 0))
    pick = jnp.concatenate([near_pick.astype(BF16), far_pick[:, CAP:]], axis=1)

    @pl.when(r > 0)
    def _():
        spread_on(lbuf, l_send, l_recv)

    for dz in (5, 6, 7, 8, -5, -6, -7):
        wait_cand(slot_of(dz))
        send_cand(slot_of(dz), partner, y * NZ)

    @pl.when((y == 0) & (z > 0))
    def _():
        copy(zbuf, zbuf, z_send.at[0], z_recv.at[0], partner).wait_recv()
        pass_on(zbuf.at[1]).start()

    wait_shards(pbuf, p_recv.at[0], 14)

    @pl.when(r == 0)
    def _():
        for i in range(1, 16):
            lbuf[(c + i) % 16] = pbuf[(c + i) % 16]

    panel_t = pbuf[...].reshape(BLOCK, BLOCK)
    for a in range(0, BLOCK, 128):
        for b in range(0, BLOCK, 128):
            straight[b : b + 128, a : a + 128] = panel_t[a : a + 128, b : b + 128].astype(F32).T.astype(BF16)

    @pl.when(r > 0)
    def _():
        wait_shards(lbuf, l_recv.at[0], 14)

    diagonal_t = lbuf[...].reshape(BLOCK, BLOCK)

    def block(a, b):
        return diagonal_t[128 * b : 128 * b + 128, 128 * a : 128 * a + 128].astype(F32).T.astype(BF16)

    first, second = lower_inverse(block)
    corner = jnp.concatenate(
        [jnp.concatenate([block(2, 0), block(2, 1)], 1), jnp.concatenate([block(3, 0), block(3, 1)], 1)], 0
    )
    first_high, first_low = split(first)
    second_high, second_low = split(second)

    theirs = cand.at[pl.ds((1 - y) * NZ, NZ)]
    copy(theirs, theirs, c_send.at[0], c_recv.at[(1 - y) * NZ], partner).wait_recv()
    top = dot(pick, cand[...].reshape(32 * CAP, 256))
    half = top[:256].astype(BF16)
    upper1 = dot(first_high, half) + dot(first_low, half)
    high1, low1 = split(upper1)
    high2, low2 = split(top[256:] - (dot(corner, high1) + dot(corner, low1)))
    upper2 = dot(second_high, high2) + dot(second_high, low2) + dot(second_low, high2)
    upper = jnp.concatenate([high1, upper2.astype(BF16)], axis=0)

    @pl.when(r > 0)
    def _():
        @pl.when(y == 1)
        def _():
            pass_on(zbuf.at[1]).wait_recv()

        last = jnp.where(later_row > 0, 0, mine)
        place = dot_nt(local_hit, ones(last > 0))
        moved = dot(place.astype(BF16), zbuf[0])
        hit = jnp.sum(place, axis=1, keepdims=True) > 0
        product = dot(straight[...], upper)
        out[...] = (jnp.where(hit, moved, slab[...].astype(F32)) - product).astype(BF16)

    @pl.when(r == 0)
    def _():
        out[...] = upper

    every = cand.at[pl.ds(0, 31)]
    copy(every, every, c_send.at[0], c_recv.at[0], partner).wait_send()
    spread_done(pbuf, p_send, p_recv)

    @pl.when(r > 0)
    def _():
        spread_done(lbuf, l_send, l_recv)

    @pl.when(z == 0)
    def _():
        for dz in range(1, NZ):
            copy(lbuf.at[c], lbuf.at[c], lz_send.at[dz], l_recv.at[c], partner).wait_send()

    @pl.when(r == 0)
    def _():
        copy(lbuf.at[c], lbuf.at[c], lz_send.at[0], l_recv.at[c], partner).wait_send()
        for dz in range(1, NZ):
            copy(zsend.at[dz], zbuf, z_send.at[dz], z_recv.at[0], at(dz)).wait_send()

    @pl.when(y == 0)
    def _():
        pass_on(zbuf.at[1]).wait_send()


def local(slab, panels, pivots):
    vmem = pl.BlockSpec(memory_space=pltpu.VMEM)
    dma = pltpu.SemaphoreType.DMA
    out, over = pl.pallas_call(
        kernel,
        out_shape=(jax.ShapeDtypeStruct(slab.shape, BF16), jax.ShapeDtypeStruct((1, 1), I32)),
        in_specs=[vmem] * 3,
        out_specs=(vmem, pl.BlockSpec(memory_space=pltpu.SMEM)),
        scratch_shapes=[
            pltpu.VMEM((32, CAP, 256), BF16),
            pltpu.VMEM((16, 32, BLOCK), BF16),
            pltpu.VMEM((16, 32, BLOCK), BF16),
            pltpu.VMEM((2, CAP, 256), BF16),
            pltpu.VMEM((NZ, 2, CAP, 256), BF16),
            pltpu.VMEM((BLOCK, BLOCK), BF16),
            dma((32,)), dma((32,)), dma((16,)), dma((16,)), dma((16,)), dma((16,)), dma((16,)), dma((16,)), dma((2,)),
            pltpu.SemaphoreType.REGULAR((16,)),
        ],
        compiler_params=pltpu.CompilerParams(collective_id=0, has_side_effects=True),
        name="lu_update",
    )(slab, jnp.transpose(panels[0]), pivots)
    return lax.cond(over[0, 0] >= CAP, general, lambda *_: out, slab, panels, pivots)


def solution(mesh):
    in_specs = (P("prow", "pcol"), P(None, "prow", "pcol"), P())
    out_specs = P("prow", "pcol")
    return jax.shard_map(local, mesh=mesh, in_specs=in_specs, out_specs=out_specs, check_vma=False)
```

```python
import jax
import jax.numpy as jnp
from jax import lax
from jax.experimental import pallas as pl
from jax.experimental.pallas import tpu as pltpu
from jax.sharding import PartitionSpec as P

BLOCK = 512
CAP = 32
NZ = 16
MESH = pl.DeviceIdType.MESH
F32 = jnp.float32
BF16 = jnp.bfloat16
I32 = jnp.int32


def general(slab, panels, pivots):
    def gathered(x, axis):
        n = lax.axis_size(axis)
        return lax.all_to_all(jnp.broadcast_to(x[None], (n, *x.shape)), axis, 0, 0, tiled=True)

    rows_local, cols_local = slab.shape
    row_start = lax.axis_index("prow") * rows_local
    global_rows = row_start + jnp.arange(rows_local, dtype=I32)
    steps = jnp.arange(BLOCK, dtype=I32)
    pivot_row = pivots[0]
    earlier = steps[:, None] < steps[None, :]
    hit = (pivot_row[:, None] == steps[None, :]) & earlier
    parent = jnp.max(jnp.where(hit, steps[:, None], -1), axis=0)
    pointer = jnp.where(parent >= 0, parent, steps)
    pointer = lax.fori_loop(0, 10, lambda _, p: jnp.take(p, p), pointer)
    same = (pivot_row[:, None] == pivot_row[None, :]) & earlier
    latest = jnp.max(jnp.where(same, steps[:, None], -1), axis=0)
    top_source = jnp.where(latest >= 0, jnp.take(pointer, jnp.clip(latest, 0, BLOCK - 1)), pivot_row)
    local_source = top_source - row_start
    is_mine = (local_source >= 0) & (local_source < rows_local)
    fetched = jnp.take(slab, jnp.clip(local_source, 0, rows_local - 1), axis=0)
    picked = jnp.where(is_mine[:, None], fetched, jnp.zeros_like(fetched))
    top = gathered(picked, "prow").astype(F32).sum(axis=0)
    old_top = gathered(slab, "prow")[0]
    diagonal = gathered(gathered(panels[0], "prow")[0], "pcol")
    diagonal = jnp.moveaxis(diagonal, 0, 1).reshape(BLOCK, BLOCK).astype(F32)
    upper = jax.scipy.linalg.solve_triangular(diagonal, top, lower=True, unit_diagonal=True).astype(BF16)
    match = global_rows[:, None] == pivot_row[None, :]
    last_hit = jnp.max(jnp.where(match, steps[None, :], -1), axis=1)
    displaced = (last_hit >= 0) & (global_rows >= BLOCK)
    moved = jnp.take(old_top, jnp.take(pointer, jnp.clip(last_hit, 0, BLOCK - 1)), axis=0)
    swapped = jnp.where(displaced[:, None], moved, slab)
    whole = jnp.moveaxis(gathered(panels[0], "pcol"), 0, 1).reshape(rows_local, BLOCK)
    product = jnp.dot(whole, upper, preferred_element_type=F32)
    updated = (swapped.astype(F32) - product).astype(BF16)
    return jnp.where(row_start == 0, upper, updated)


def iota(shape, dim):
    return lax.broadcasted_iota(I32, shape, dim)


def ones(mask):
    return jnp.where(mask, 1.0, 0.0).astype(BF16)


def dot(a, b):
    return jnp.dot(a, b, preferred_element_type=F32)


def dot_nt(a, b):
    return lax.dot_general(a, b, (((1,), (1,)), ((), ())), preferred_element_type=F32)


def column(row):
    n = row.shape[1]
    blocks = [jnp.broadcast_to(row[:, i : i + 128], (128, 128)).astype(F32).T[:, :1] for i in range(0, n, 128)]
    return jnp.concatenate(blocks, axis=0).astype(I32)


def split(x):
    high = x.astype(BF16)
    return high, (x - high.astype(F32)).astype(BF16)


def dot_f32(a, b):
    a_parts = (a,) if a.dtype == BF16 else split(a)
    b_parts = (b,) if b.dtype == BF16 else split(b)
    total = dot(a_parts[0], b_parts[0])
    if len(b_parts) > 1:
        total += dot(a_parts[0], b_parts[1])
    if len(a_parts) > 1:
        total += dot(a_parts[1], b_parts[0])
    return total


def lower_inverse(block):
    i, j = iota((128, 128), 0), iota((128, 128), 1)
    eye = jnp.where(i == j, 1.0, 0.0)
    inv, full, power = [], [], []
    for d in range(4):
        full.append(block(d, d))
        n = jnp.where((i // 16 == j // 16) & (i > j), full[d].astype(F32), 0.0)
        inv.append(eye - n)
        power.append(n.astype(BF16))
    for _ in range(3):
        for d in range(4):
            power[d] = dot_f32(power[d], power[d])
        for d in range(4):
            inv[d] = inv[d] + dot_f32(inv[d], power[d])
    for size in (16, 32, 64):
        off = (i // (2 * size) == j // (2 * size)) & (i // size > j // size)
        step = [dot_f32(jnp.where(off, full[d].astype(F32), 0.0).astype(BF16), inv[d]) for d in range(4)]
        for d in range(4):
            inv[d] = inv[d] - dot_f32(inv[d], step[d])
    zero = jnp.zeros((128, 128), F32)
    halves = []
    for d in (0, 2):
        lower = -dot_f32(inv[d + 1], dot_f32(block(d + 1, d), inv[d]))
        halves.append(jnp.concatenate([jnp.concatenate([inv[d], zero], 1), jnp.concatenate([lower, inv[d + 1]], 1)], 0))
    return halves


def kernel(
    slab, panel, pivot, out, over,
    cand, pbuf, lbuf, zbuf, zsend, straight,
    c_send, c_recv, p_send, p_recv, l_send, l_recv, lz_send, z_send, z_recv, ready,
):
    r, c = lax.axis_index("prow"), lax.axis_index("pcol")
    y, z = r // NZ, r % NZ

    def ring(dz):
        return (z + dz + NZ) % NZ

    def at(dz):
        return (y * NZ + ring(dz), c)

    partner = ((1 - y) * NZ + z, c)

    across = (c + 8) % 16

    def peer(i):
        return (r, (c // 8) * 8 + (c + i) % 8) if i < 8 else (r, across)

    def copy(src, dst, send, recv, device):
        return pltpu.make_async_remote_copy(
            src_ref=src, dst_ref=dst, send_sem=send, recv_sem=recv, device_id=device, device_id_type=MESH
        )

    near = (4, -4, 3, -3, 2, -2, 1, -1)
    barrier = pltpu.get_barrier_semaphore()

    def hello(device):
        pl.semaphore_signal(barrier, inc=1, device_id=device, device_id_type=MESH)

    hello(partner)
    for i in range(1, 9):
        hello(peer(i))
    for dz in near:

        @pl.when(ring(dz) > z)
        def _(dz=dz):
            hello(at(dz))

    @pl.when(z == 0)
    def _():
        for dz in range(5, 12):
            hello(at(dz))

    pl.semaphore_wait(
        barrier, 9 + jnp.minimum(z, 4) + jnp.maximum(z - 11, 0) + jnp.where((z > 4) & (z < 12), 1, 0)
    )

    def announce(device):
        pl.semaphore_signal(ready.at[z], inc=1, device_id=device, device_id_type=MESH)

    @pl.when((z > 4) & (z < 12) & (z != 9) & (z != 10))
    def _():
        announce((y * NZ, c))

    for dz in near:

        @pl.when(ring(dz) < z)
        def _(dz=dz):
            announce(at(dz))

    def send_cand(slot, device, recv=None):
        copy(cand.at[slot], cand.at[slot], c_send.at[0], c_recv.at[slot if recv is None else recv], device).start()

    def wait_cand(slot):
        copy(cand.at[slot], cand.at[slot], c_send.at[0], c_recv.at[slot], partner).wait_recv()

    def slot_of(dz):
        return y * NZ + ring(dz)

    def send_shard(n, device):
        copy(lbuf.at[c], lbuf.at[c], lz_send.at[n], l_recv.at[2], device).start()

    def wait_shards(buf, sem, count):
        some = buf.at[pl.ds(0, count)]
        copy(some, some, p_send.at[0], sem, partner).wait_recv()

    @pl.when(r == 0)
    def _():
        copy(panel, lbuf.at[c], lz_send.at[0], l_recv.at[2], partner).start()
        lbuf[c] = panel[...]

    p_row = pivot[...]
    b_row = p_row // BLOCK
    far_row = p_row >= BLOCK
    before = ones(iota((BLOCK, BLOCK), 0) < iota((BLOCK, BLOCK), 1))
    in_block = iota((32, BLOCK), 0) == b_row
    counts = dot(ones(in_block), before)
    rank_row = jnp.sum(jnp.where(in_block, counts, 0.0), axis=0, keepdims=True).astype(I32)
    slots = iota((CAP, BLOCK), 0)
    mine = jnp.where((b_row == r) & far_row, 1, 0) * jnp.where(rank_row == slots, 1, 0)
    local_hit = ones(iota((BLOCK, BLOCK), 0) + r * BLOCK == p_row)

    def top_slots():
        p_col = column(p_row)
        later = (p_col == p_row) & (iota((BLOCK, BLOCK), 0) > iota((BLOCK, BLOCK), 1))
        later_row = jnp.max(jnp.where(later, 1, 0), axis=0, keepdims=True)
        hit_row = jnp.max(jnp.where(p_col == iota((BLOCK, BLOCK), 1), 1, 0), axis=0, keepdims=True)
        goes_on = ones((p_row < BLOCK) | (later_row > 0))
        next_goes_on = dot(goes_on, ones(iota((BLOCK, BLOCK), 0) == p_row))
        stays_row = ones((hit_row > 0) | (later_row > 0) | (next_goes_on > 0))
        return p_col, later_row, stays_row, dot(stays_row, before).astype(I32)

    slot_row = jnp.where(far_row, b_row * CAP + rank_row, -1)

    def chain_roots():
        k, j = iota((BLOCK, BLOCK), 0), iota((BLOCK, BLOCK), 1)
        parent = jnp.max(jnp.where((p_row == k) & (j < k), j, -1), axis=1, keepdims=True)
        a = ones(jnp.where(parent >= 0, parent, iota((BLOCK, 1), 0)) == j)
        return lax.fori_loop(0, 9, lambda _, a: dot(a, a).astype(BF16), a)

    @pl.when(r > 0)
    def _():
        pack = dot_nt(ones(mine > 0), local_hit)
        cand[r] = dot(pack.astype(BF16), slab[...]).astype(BF16)

    @pl.when(r == 0)
    def _():
        _, _, stays, rank0 = top_slots()
        cand[r] = dot(ones((rank0 == slots) & (stays > 0)), slab[...]).astype(BF16)

    for dz in near:

        @pl.when(ring(dz) < z)
        def _(dz=dz):
            send_cand(r, at(dz))

    send_cand(r, partner, y * NZ)

    def root_sends(steps, shard, slot):
        @pl.when(z == 0)
        def _():
            for dz in steps:
                if slot is not None:
                    pl.semaphore_wait(ready.at[dz], 1)
                if slot:
                    send_cand(r, at(dz))
                if shard:
                    send_shard(dz, at(dz))

    @pl.when(r == NZ)
    def _():
        wait_shards(lbuf, l_recv.at[2], 1)

    root_sends((1, 2, 3, 4), True, True)
    root_sends((15, 14, 13, 12), False, True)
    root_sends((5, 6, 7), True, False)
    root_sends((11, 8), True, False)
    root_sends((12, 13, 14, 15), True, None)

    @pl.when(z > 4)
    def _():
        for dz in near:

            @pl.when(ring(dz) > z)
            def _(dz=dz):
                pl.semaphore_wait(ready.at[ring(dz)], 1)
                send_cand(r, at(dz))

    def spread(src, buf, send, recv):
        for i in range(8, 0, -1):
            copy(src, buf.at[c], send.at[0], recv.at[1 if i == 8 else 0], peer(i)).start()

    def spread_on(buf, send, recv):
        wait_shards(buf, recv.at[1], 1)
        for i in range(1, 8):
            copy(buf.at[across], buf.at[across], send.at[0], recv.at[0], peer(i)).start()

    def spread_done(buf, send, recv):
        some = buf.at[pl.ds(0, 15)]
        copy(some, some, send.at[0], recv.at[0], partner).wait_send()

    pbuf[c] = panel[...]
    spread(panel, pbuf, p_send, p_recv)

    def spread_shard():
        spread(lbuf.at[c], lbuf, l_send, l_recv)

    @pl.when(r == NZ)
    def _():
        spread_shard()

    @pl.when((z > 0) & (z < 5))
    def _():
        for dz in (1, 2, 3, 4, -1, -2, -3, -4):

            @pl.when(ring(dz) > z)
            def _(dz=dz):
                pl.semaphore_wait(ready.at[ring(dz)], 1)
                send_cand(r, at(dz))

        wait_shards(lbuf, l_recv.at[2], 1)
        spread_shard()

    @pl.when(r == 0)
    def _():
        content = dot(chain_roots(), slab[...]).astype(BF16)
        for q in range(0, 32, 4):
            pick = ones(slot_row == iota((4 * CAP, BLOCK), 0) + q * CAP)
            zsend[q % NZ : q % NZ + 4, q // NZ] = dot(pick, content).astype(BF16).reshape(4, CAP, 256)

    p_col, later_row, stays_row, rank0_row = top_slots()
    kk = iota((BLOCK, BLOCK), 0)
    jj = iota((BLOCK, BLOCK), 1)

    for dz in (4, 3, 2, 1):
        wait_cand(slot_of(dz))
        send_cand(slot_of(dz), at(-4))
        wait_cand(slot_of(-dz))
        if dz < 4:
            send_cand(slot_of(-dz), at(4))
    for dz in near:
        send_cand(slot_of(dz), partner, y * NZ)

    spread_on(pbuf, p_send, p_recv)

    def pass_on(rows):
        return copy(rows, zbuf.at[0], z_send.at[0], z_recv.at[0], partner)

    @pl.when(r == 0)
    def _():
        for dz in range(1, NZ):
            copy(zsend.at[dz], zbuf, z_send.at[dz], z_recv.at[0], at(dz)).start()
        pass_on(zsend.at[0, 1]).start()

    @pl.when(z > 4)
    def _():
        wait_shards(lbuf, l_recv.at[2], 1)

        @pl.when(z == 8)
        def _():
            send_shard(1, at(1))
            send_shard(2, at(2))

        spread_shard()

    chain = chain_roots()
    full = jnp.max(jnp.where(far_row, rank_row, 0), axis=1, keepdims=True)
    full0 = jnp.max(jnp.where(stays_row > 0, rank0_row, 0), axis=1, keepdims=True)
    over[0, 0] = jnp.max(jnp.maximum(full, full0))
    latest = jnp.max(jnp.where((p_col == p_row) & (jj < kk), jj, -1), axis=1, keepdims=True)
    source = dot(ones(latest == jj), chain) + jnp.where((latest < 0) & (p_col == jj), 1.0, 0.0)
    rank0_col = column(jnp.where(stays_row > 0, rank0_row, -1))
    near_pick = dot(source.astype(BF16), ones(rank0_col == iota((BLOCK, CAP), 1)))
    slot_col = column(slot_row)
    far_pick = ones((slot_col == iota((BLOCK, 32 * CAP), 1)) & (latest < 0))
    pick = jnp.concatenate([near_pick.astype(BF16), far_pick[:, CAP:]], axis=1)

    @pl.when(r > 0)
    def _():
        spread_on(lbuf, l_send, l_recv)

    for dz in (5, 6, 7, 8, -5, -6, -7):
        wait_cand(slot_of(dz))
        send_cand(slot_of(dz), partner, y * NZ)

    @pl.when((y == 0) & (z > 0))
    def _():
        copy(zbuf, zbuf, z_send.at[0], z_recv.at[0], partner).wait_recv()
        pass_on(zbuf.at[1]).start()

    wait_shards(pbuf, p_recv.at[0], 14)

    @pl.when(r == 0)
    def _():
        for i in range(1, 16):
            lbuf[(c + i) % 16] = pbuf[(c + i) % 16]

    panel_t = pbuf[...].reshape(BLOCK, BLOCK)
    for a in range(0, BLOCK, 128):
        for b in range(0, BLOCK, 128):
            straight[b : b + 128, a : a + 128] = panel_t[a : a + 128, b : b + 128].astype(F32).T.astype(BF16)

    @pl.when(r > 0)
    def _():
        wait_shards(lbuf, l_recv.at[0], 14)

    diagonal_t = lbuf[...].reshape(BLOCK, BLOCK)

    def block(a, b):
        return diagonal_t[128 * b : 128 * b + 128, 128 * a : 128 * a + 128].astype(F32).T.astype(BF16)

    first, second = lower_inverse(block)
    corner = jnp.concatenate(
        [jnp.concatenate([block(2, 0), block(2, 1)], 1), jnp.concatenate([block(3, 0), block(3, 1)], 1)], 0
    )
    first_high, first_low = split(first)
    second_high, second_low = split(second)

    theirs = cand.at[pl.ds((1 - y) * NZ, NZ)]
    copy(theirs, theirs, c_send.at[0], c_recv.at[(1 - y) * NZ], partner).wait_recv()
    top = dot(pick, cand[...].reshape(32 * CAP, 256))
    half = top[:256].astype(BF16)
    upper1 = dot(first_high, half) + dot(first_low, half)
    high1, low1 = split(upper1)
    high2, low2 = split(top[256:] - (dot(corner, high1) + dot(corner, low1)))
    upper2 = dot(second_high, high2) + dot(second_high, low2) + dot(second_low, high2)
    upper = jnp.concatenate([high1, upper2.astype(BF16)], axis=0)

    @pl.when(r > 0)
    def _():
        @pl.when(y == 1)
        def _():
            pass_on(zbuf.at[1]).wait_recv()

        last = jnp.where(later_row > 0, 0, mine)
        place = dot_nt(local_hit, ones(last > 0))
        moved = dot(place.astype(BF16), zbuf[0])
        hit = jnp.sum(place, axis=1, keepdims=True) > 0
        product = dot(straight[...], upper)
        out[...] = (jnp.where(hit, moved, slab[...].astype(F32)) - product).astype(BF16)

    @pl.when(r == 0)
    def _():
        out[...] = upper

    every = cand.at[pl.ds(0, 31)]
    copy(every, every, c_send.at[0], c_recv.at[0], partner).wait_send()
    spread_done(pbuf, p_send, p_recv)

    @pl.when(r > 0)
    def _():
        spread_done(lbuf, l_send, l_recv)

    @pl.when(z == 0)
    def _():
        for dz in (1, 2, 3, 4, 5, 6, 7, 8, 11, 12, 13, 14, 15):
            copy(lbuf.at[c], lbuf.at[c], lz_send.at[dz], l_recv.at[c], partner).wait_send()

    @pl.when(z == 8)
    def _():
        for dz in (1, 2):
            copy(lbuf.at[c], lbuf.at[c], lz_send.at[dz], l_recv.at[c], partner).wait_send()

    @pl.when(r == 0)
    def _():
        copy(lbuf.at[c], lbuf.at[c], lz_send.at[0], l_recv.at[c], partner).wait_send()
        for dz in range(1, NZ):
            copy(zsend.at[dz], zbuf, z_send.at[dz], z_recv.at[0], at(dz)).wait_send()

    @pl.when(y == 0)
    def _():
        pass_on(zbuf.at[1]).wait_send()


def local(slab, panels, pivots):
    vmem = pl.BlockSpec(memory_space=pltpu.VMEM)
    dma = pltpu.SemaphoreType.DMA
    out, over = pl.pallas_call(
        kernel,
        out_shape=(jax.ShapeDtypeStruct(slab.shape, BF16), jax.ShapeDtypeStruct((1, 1), I32)),
        in_specs=[vmem] * 3,
        out_specs=(vmem, pl.BlockSpec(memory_space=pltpu.SMEM)),
        scratch_shapes=[
            pltpu.VMEM((32, CAP, 256), BF16),
            pltpu.VMEM((16, 32, BLOCK), BF16),
            pltpu.VMEM((16, 32, BLOCK), BF16),
            pltpu.VMEM((2, CAP, 256), BF16),
            pltpu.VMEM((NZ, 2, CAP, 256), BF16),
            pltpu.VMEM((BLOCK, BLOCK), BF16),
            dma((32,)), dma((32,)), dma((16,)), dma((16,)), dma((16,)), dma((16,)), dma((16,)), dma((16,)), dma((2,)),
            pltpu.SemaphoreType.REGULAR((16,)),
        ],
        compiler_params=pltpu.CompilerParams(collective_id=0, has_side_effects=True),
        name="lu_update",
    )(slab, jnp.transpose(panels[0]), pivots)
    return lax.cond(over[0, 0] >= CAP, general, lambda *_: out, slab, panels, pivots)


def solution(mesh):
    in_specs = (P("prow", "pcol"), P(None, "prow", "pcol"), P())
    out_specs = P("prow", "pcol")
    return jax.shard_map(local, mesh=mesh, in_specs=in_specs, out_specs=out_specs, check_vma=False)
```

```python
import jax
import jax.numpy as jnp
from jax import lax
from jax.experimental import pallas as pl
from jax.experimental.pallas import tpu as pltpu
from jax.sharding import PartitionSpec as P

BLOCK = 512
CAP = 32
NZ = 16
MESH = pl.DeviceIdType.MESH
F32 = jnp.float32
BF16 = jnp.bfloat16
I32 = jnp.int32


def general(slab, panels, pivots):
    def gathered(x, axis):
        n = lax.axis_size(axis)
        return lax.all_to_all(jnp.broadcast_to(x[None], (n, *x.shape)), axis, 0, 0, tiled=True)

    rows_local, cols_local = slab.shape
    row_start = lax.axis_index("prow") * rows_local
    global_rows = row_start + jnp.arange(rows_local, dtype=I32)
    steps = jnp.arange(BLOCK, dtype=I32)
    pivot_row = pivots[0]
    earlier = steps[:, None] < steps[None, :]
    hit = (pivot_row[:, None] == steps[None, :]) & earlier
    parent = jnp.max(jnp.where(hit, steps[:, None], -1), axis=0)
    pointer = jnp.where(parent >= 0, parent, steps)
    pointer = lax.fori_loop(0, 10, lambda _, p: jnp.take(p, p), pointer)
    same = (pivot_row[:, None] == pivot_row[None, :]) & earlier
    latest = jnp.max(jnp.where(same, steps[:, None], -1), axis=0)
    top_source = jnp.where(latest >= 0, jnp.take(pointer, jnp.clip(latest, 0, BLOCK - 1)), pivot_row)
    local_source = top_source - row_start
    is_mine = (local_source >= 0) & (local_source < rows_local)
    fetched = jnp.take(slab, jnp.clip(local_source, 0, rows_local - 1), axis=0)
    picked = jnp.where(is_mine[:, None], fetched, jnp.zeros_like(fetched))
    top = gathered(picked, "prow").astype(F32).sum(axis=0)
    old_top = gathered(slab, "prow")[0]
    diagonal = gathered(gathered(panels[0], "prow")[0], "pcol")
    diagonal = jnp.moveaxis(diagonal, 0, 1).reshape(BLOCK, BLOCK).astype(F32)
    upper = jax.scipy.linalg.solve_triangular(diagonal, top, lower=True, unit_diagonal=True).astype(BF16)
    match = global_rows[:, None] == pivot_row[None, :]
    last_hit = jnp.max(jnp.where(match, steps[None, :], -1), axis=1)
    displaced = (last_hit >= 0) & (global_rows >= BLOCK)
    moved = jnp.take(old_top, jnp.take(pointer, jnp.clip(last_hit, 0, BLOCK - 1)), axis=0)
    swapped = jnp.where(displaced[:, None], moved, slab)
    whole = jnp.moveaxis(gathered(panels[0], "pcol"), 0, 1).reshape(rows_local, BLOCK)
    product = jnp.dot(whole, upper, preferred_element_type=F32)
    updated = (swapped.astype(F32) - product).astype(BF16)
    return jnp.where(row_start == 0, upper, updated)


def iota(shape, dim):
    return lax.broadcasted_iota(I32, shape, dim)


def ones(mask):
    return jnp.where(mask, 1.0, 0.0).astype(BF16)


def dot(a, b):
    return jnp.dot(a, b, preferred_element_type=F32)


def dot_nt(a, b):
    return lax.dot_general(a, b, (((1,), (1,)), ((), ())), preferred_element_type=F32)


def column(row):
    n = row.shape[1]
    blocks = [jnp.broadcast_to(row[:, i : i + 128], (128, 128)).astype(F32).T[:, :1] for i in range(0, n, 128)]
    return jnp.concatenate(blocks, axis=0).astype(I32)


def split(x):
    high = x.astype(BF16)
    return high, (x - high.astype(F32)).astype(BF16)


def dot_f32(a, b):
    a_parts = (a,) if a.dtype == BF16 else split(a)
    b_parts = (b,) if b.dtype == BF16 else split(b)
    total = dot(a_parts[0], b_parts[0])
    if len(b_parts) > 1:
        total += dot(a_parts[0], b_parts[1])
    if len(a_parts) > 1:
        total += dot(a_parts[1], b_parts[0])
    return total


def lower_inverse(block):
    i, j = iota((128, 128), 0), iota((128, 128), 1)
    eye = jnp.where(i == j, 1.0, 0.0)
    inv, full, power = [], [], []
    for d in range(4):
        full.append(block(d, d))
        n = jnp.where((i // 16 == j // 16) & (i > j), full[d].astype(F32), 0.0)
        inv.append(eye - n)
        power.append(n.astype(BF16))
    for _ in range(3):
        for d in range(4):
            power[d] = dot_f32(power[d], power[d])
        for d in range(4):
            inv[d] = inv[d] + dot_f32(inv[d], power[d])
    for size in (16, 32, 64):
        off = (i // (2 * size) == j // (2 * size)) & (i // size > j // size)
        step = [dot_f32(jnp.where(off, full[d].astype(F32), 0.0).astype(BF16), inv[d]) for d in range(4)]
        for d in range(4):
            inv[d] = inv[d] - dot_f32(inv[d], step[d])
    zero = jnp.zeros((128, 128), F32)
    halves = []
    for d in (0, 2):
        lower = -dot_f32(inv[d + 1], dot_f32(block(d + 1, d), inv[d]))
        halves.append(jnp.concatenate([jnp.concatenate([inv[d], zero], 1), jnp.concatenate([lower, inv[d + 1]], 1)], 0))
    return halves


def kernel(
    slab, panel, pivot, out, over,
    cand, pbuf, lbuf, zbuf, zsend, straight,
    c_send, c_recv, p_send, p_recv, l_send, l_recv, lz_send, z_send, z_recv, ready,
):
    r, c = lax.axis_index("prow"), lax.axis_index("pcol")
    y, z = r // NZ, r % NZ

    def ring(dz):
        return (z + dz + NZ) % NZ

    def at(dz):
        return (y * NZ + ring(dz), c)

    partner = ((1 - y) * NZ + z, c)

    across = (c + 8) % 16

    def peer(i):
        return (r, (c // 8) * 8 + (c + i) % 8) if i < 8 else (r, across)

    def copy(src, dst, send, recv, device):
        return pltpu.make_async_remote_copy(
            src_ref=src, dst_ref=dst, send_sem=send, recv_sem=recv, device_id=device, device_id_type=MESH
        )

    near = (4, -4, 3, -3, 2, -2, 1, -1)
    barrier = pltpu.get_barrier_semaphore()

    def hello(device):
        pl.semaphore_signal(barrier, inc=1, device_id=device, device_id_type=MESH)

    hello(partner)
    for i in range(1, 9):
        hello(peer(i))
    for dz in near:

        @pl.when(ring(dz) > z)
        def _(dz=dz):
            hello(at(dz))

    @pl.when(z == 0)
    def _():
        for dz in range(5, 12):
            hello(at(dz))

    pl.semaphore_wait(
        barrier, 9 + jnp.minimum(z, 4) + jnp.maximum(z - 11, 0) + jnp.where((z > 4) & (z < 12), 1, 0)
    )

    def announce(device):
        pl.semaphore_signal(ready.at[z], inc=1, device_id=device, device_id_type=MESH)

    @pl.when((z > 4) & (z < 9))
    def _():
        announce((y * NZ, c))

    for dz in near:

        @pl.when(ring(dz) < z)
        def _(dz=dz):
            announce(at(dz))

    def send_cand(slot, device, recv=None):
        copy(cand.at[slot], cand.at[slot], c_send.at[0], c_recv.at[slot if recv is None else recv], device).start()

    def wait_cand(slot):
        copy(cand.at[slot], cand.at[slot], c_send.at[0], c_recv.at[slot], partner).wait_recv()

    def slot_of(dz):
        return y * NZ + ring(dz)

    def send_shard(n, device):
        copy(lbuf.at[c], lbuf.at[c], lz_send.at[n], l_recv.at[2], device).start()

    def wait_shards(buf, sem, count):
        some = buf.at[pl.ds(0, count)]
        copy(some, some, p_send.at[0], sem, partner).wait_recv()

    @pl.when(r == 0)
    def _():
        copy(panel, lbuf.at[c], lz_send.at[0], l_recv.at[2], partner).start()
        lbuf[c] = panel[...]

    p_row = pivot[...]
    b_row = p_row // BLOCK
    far_row = p_row >= BLOCK
    before = ones(iota((BLOCK, BLOCK), 0) < iota((BLOCK, BLOCK), 1))
    in_block = iota((32, BLOCK), 0) == b_row
    counts = dot(ones(in_block), before)
    rank_row = jnp.sum(jnp.where(in_block, counts, 0.0), axis=0, keepdims=True).astype(I32)
    slots = iota((CAP, BLOCK), 0)
    mine = jnp.where((b_row == r) & far_row, 1, 0) * jnp.where(rank_row == slots, 1, 0)
    local_hit = ones(iota((BLOCK, BLOCK), 0) + r * BLOCK == p_row)

    def top_slots():
        p_col = column(p_row)
        later = (p_col == p_row) & (iota((BLOCK, BLOCK), 0) > iota((BLOCK, BLOCK), 1))
        later_row = jnp.max(jnp.where(later, 1, 0), axis=0, keepdims=True)
        hit_row = jnp.max(jnp.where(p_col == iota((BLOCK, BLOCK), 1), 1, 0), axis=0, keepdims=True)
        goes_on = ones((p_row < BLOCK) | (later_row > 0))
        next_goes_on = dot(goes_on, ones(iota((BLOCK, BLOCK), 0) == p_row))
        stays_row = ones((hit_row > 0) | (later_row > 0) | (next_goes_on > 0))
        return p_col, later_row, stays_row, dot(stays_row, before).astype(I32)

    slot_row = jnp.where(far_row, b_row * CAP + rank_row, -1)

    def chain_roots():
        k, j = iota((BLOCK, BLOCK), 0), iota((BLOCK, BLOCK), 1)
        parent = jnp.max(jnp.where((p_row == k) & (j < k), j, -1), axis=1, keepdims=True)
        a = ones(jnp.where(parent >= 0, parent, iota((BLOCK, 1), 0)) == j)
        return lax.fori_loop(0, 9, lambda _, a: dot(a, a).astype(BF16), a)

    @pl.when(r > 0)
    def _():
        pack = dot_nt(ones(mine > 0), local_hit)
        cand[r] = dot(pack.astype(BF16), slab[...]).astype(BF16)

    @pl.when(r == 0)
    def _():
        _, _, stays, rank0 = top_slots()
        cand[r] = dot(ones((rank0 == slots) & (stays > 0)), slab[...]).astype(BF16)

    for dz in near:

        @pl.when(ring(dz) < z)
        def _(dz=dz):
            send_cand(r, at(dz))

    send_cand(r, partner, y * NZ)

    def root_sends(steps, shard, slot):
        @pl.when(z == 0)
        def _():
            for dz in steps:
                if slot is not None:
                    pl.semaphore_wait(ready.at[dz], 1)
                if slot:
                    send_cand(r, at(dz))
                if shard:
                    send_shard(dz, at(dz))

    @pl.when(r == NZ)
    def _():
        wait_shards(lbuf, l_recv.at[2], 1)

    root_sends((1, 2, 3, 4), True, True)
    root_sends((15, 14, 13, 12), False, True)
    root_sends((5, 6, 7), True, False)
    root_sends((8,), True, False)
    root_sends((12, 13, 14, 15), True, None)

    @pl.when(z > 4)
    def _():
        for dz in near:

            @pl.when(ring(dz) > z)
            def _(dz=dz):
                pl.semaphore_wait(ready.at[ring(dz)], 1)
                send_cand(r, at(dz))

    def spread(src, buf, send, recv):
        for i in range(8, 0, -1):
            copy(src, buf.at[c], send.at[0], recv.at[1 if i == 8 else 0], peer(i)).start()

    def spread_on(buf, send, recv):
        wait_shards(buf, recv.at[1], 1)
        for i in range(1, 8):
            copy(buf.at[across], buf.at[across], send.at[0], recv.at[0], peer(i)).start()

    def spread_done(buf, send, recv):
        some = buf.at[pl.ds(0, 15)]
        copy(some, some, send.at[0], recv.at[0], partner).wait_send()

    pbuf[c] = panel[...]
    spread(panel, pbuf, p_send, p_recv)

    def spread_shard():
        spread(lbuf.at[c], lbuf, l_send, l_recv)

    @pl.when(r == NZ)
    def _():
        spread_shard()

    @pl.when((z > 0) & (z < 5))
    def _():
        for dz in (1, 2, 3, 4, -1, -2, -3, -4):

            @pl.when(ring(dz) > z)
            def _(dz=dz):
                pl.semaphore_wait(ready.at[ring(dz)], 1)
                send_cand(r, at(dz))

        wait_shards(lbuf, l_recv.at[2], 1)
        spread_shard()

    @pl.when(r == 0)
    def _():
        content = dot(chain_roots(), slab[...]).astype(BF16)
        for q in range(0, 32, 4):
            pick = ones(slot_row == iota((4 * CAP, BLOCK), 0) + q * CAP)
            zsend[q % NZ : q % NZ + 4, q // NZ] = dot(pick, content).astype(BF16).reshape(4, CAP, 256)

    p_col, later_row, stays_row, rank0_row = top_slots()
    kk = iota((BLOCK, BLOCK), 0)
    jj = iota((BLOCK, BLOCK), 1)

    for dz in (4, 3, 2, 1):
        wait_cand(slot_of(dz))
        send_cand(slot_of(dz), at(-4))
        wait_cand(slot_of(-dz))
        if dz < 4:
            send_cand(slot_of(-dz), at(4))
    for dz in near:
        send_cand(slot_of(dz), partner, y * NZ)

    spread_on(pbuf, p_send, p_recv)

    def pass_on(rows):
        return copy(rows, zbuf.at[0], z_send.at[0], z_recv.at[0], partner)

    @pl.when(r == 0)
    def _():
        for dz in range(1, NZ):
            copy(zsend.at[dz], zbuf, z_send.at[dz], z_recv.at[0], at(dz)).start()
        pass_on(zsend.at[0, 1]).start()

    @pl.when(z > 4)
    def _():
        wait_shards(lbuf, l_recv.at[2], 1)

        @pl.when(z == 8)
        def _():
            send_shard(1, at(1))
            send_shard(2, at(2))
            send_shard(3, at(3))

        spread_shard()

    chain = chain_roots()
    full = jnp.max(jnp.where(far_row, rank_row, 0), axis=1, keepdims=True)
    full0 = jnp.max(jnp.where(stays_row > 0, rank0_row, 0), axis=1, keepdims=True)
    over[0, 0] = jnp.max(jnp.maximum(full, full0))
    latest = jnp.max(jnp.where((p_col == p_row) & (jj < kk), jj, -1), axis=1, keepdims=True)
    source = dot(ones(latest == jj), chain) + jnp.where((latest < 0) & (p_col == jj), 1.0, 0.0)
    rank0_col = column(jnp.where(stays_row > 0, rank0_row, -1))
    near_pick = dot(source.astype(BF16), ones(rank0_col == iota((BLOCK, CAP), 1)))
    slot_col = column(slot_row)
    far_pick = ones((slot_col == iota((BLOCK, 32 * CAP), 1)) & (latest < 0))
    pick = jnp.concatenate([near_pick.astype(BF16), far_pick[:, CAP:]], axis=1)

    @pl.when(r > 0)
    def _():
        spread_on(lbuf, l_send, l_recv)

    for dz in (5, 6, 7, 8, -5, -6, -7):
        wait_cand(slot_of(dz))
        send_cand(slot_of(dz), partner, y * NZ)

    @pl.when((y == 0) & (z > 0))
    def _():
        copy(zbuf, zbuf, z_send.at[0], z_recv.at[0], partner).wait_recv()
        pass_on(zbuf.at[1]).start()

    wait_shards(pbuf, p_recv.at[0], 14)

    @pl.when(r == 0)
    def _():
        for i in range(1, 16):
            lbuf[(c + i) % 16] = pbuf[(c + i) % 16]

    panel_t = pbuf[...].reshape(BLOCK, BLOCK)
    for a in range(0, BLOCK, 128):
        for b in range(0, BLOCK, 128):
            straight[b : b + 128, a : a + 128] = panel_t[a : a + 128, b : b + 128].astype(F32).T.astype(BF16)

    @pl.when(r > 0)
    def _():
        wait_shards(lbuf, l_recv.at[0], 14)

    diagonal_t = lbuf[...].reshape(BLOCK, BLOCK)

    def block(a, b):
        return diagonal_t[128 * b : 128 * b + 128, 128 * a : 128 * a + 128].astype(F32).T.astype(BF16)

    first, second = lower_inverse(block)
    corner = jnp.concatenate(
        [jnp.concatenate([block(2, 0), block(2, 1)], 1), jnp.concatenate([block(3, 0), block(3, 1)], 1)], 0
    )
    first_high, first_low = split(first)
    second_high, second_low = split(second)

    theirs = cand.at[pl.ds((1 - y) * NZ, NZ)]
    copy(theirs, theirs, c_send.at[0], c_recv.at[(1 - y) * NZ], partner).wait_recv()
    top = dot(pick, cand[...].reshape(32 * CAP, 256))
    half = top[:256].astype(BF16)
    upper1 = dot(first_high, half) + dot(first_low, half)
    high1, low1 = split(upper1)
    high2, low2 = split(top[256:] - (dot(corner, high1) + dot(corner, low1)))
    upper2 = dot(second_high, high2) + dot(second_high, low2) + dot(second_low, high2)
    upper = jnp.concatenate([high1, upper2.astype(BF16)], axis=0)

    @pl.when(r > 0)
    def _():
        @pl.when(y == 1)
        def _():
            pass_on(zbuf.at[1]).wait_recv()

        last = jnp.where(later_row > 0, 0, mine)
        place = dot_nt(local_hit, ones(last > 0))
        moved = dot(place.astype(BF16), zbuf[0])
        hit = jnp.sum(place, axis=1, keepdims=True) > 0
        product = dot(straight[...], upper)
        out[...] = (jnp.where(hit, moved, slab[...].astype(F32)) - product).astype(BF16)

    @pl.when(r == 0)
    def _():
        out[...] = upper

    every = cand.at[pl.ds(0, 31)]
    copy(every, every, c_send.at[0], c_recv.at[0], partner).wait_send()
    spread_done(pbuf, p_send, p_recv)

    @pl.when(r > 0)
    def _():
        spread_done(lbuf, l_send, l_recv)

    @pl.when(z == 0)
    def _():
        for dz in (1, 2, 3, 4, 5, 6, 7, 8, 12, 13, 14, 15):
            copy(lbuf.at[c], lbuf.at[c], lz_send.at[dz], l_recv.at[c], partner).wait_send()

    @pl.when(z == 8)
    def _():
        for dz in (1, 2, 3):
            copy(lbuf.at[c], lbuf.at[c], lz_send.at[dz], l_recv.at[c], partner).wait_send()

    @pl.when(r == 0)
    def _():
        copy(lbuf.at[c], lbuf.at[c], lz_send.at[0], l_recv.at[c], partner).wait_send()
        for dz in range(1, NZ):
            copy(zsend.at[dz], zbuf, z_send.at[dz], z_recv.at[0], at(dz)).wait_send()

    @pl.when(y == 0)
    def _():
        pass_on(zbuf.at[1]).wait_send()


def local(slab, panels, pivots):
    vmem = pl.BlockSpec(memory_space=pltpu.VMEM)
    dma = pltpu.SemaphoreType.DMA
    out, over = pl.pallas_call(
        kernel,
        out_shape=(jax.ShapeDtypeStruct(slab.shape, BF16), jax.ShapeDtypeStruct((1, 1), I32)),
        in_specs=[vmem] * 3,
        out_specs=(vmem, pl.BlockSpec(memory_space=pltpu.SMEM)),
        scratch_shapes=[
            pltpu.VMEM((32, CAP, 256), BF16),
            pltpu.VMEM((16, 32, BLOCK), BF16),
            pltpu.VMEM((16, 32, BLOCK), BF16),
            pltpu.VMEM((2, CAP, 256), BF16),
            pltpu.VMEM((NZ, 2, CAP, 256), BF16),
            pltpu.VMEM((BLOCK, BLOCK), BF16),
            dma((32,)), dma((32,)), dma((16,)), dma((16,)), dma((16,)), dma((16,)), dma((16,)), dma((16,)), dma((2,)),
            pltpu.SemaphoreType.REGULAR((16,)),
        ],
        compiler_params=pltpu.CompilerParams(collective_id=0, has_side_effects=True),
        name="lu_update",
    )(slab, jnp.transpose(panels[0]), pivots)
    return lax.cond(over[0, 0] >= CAP, general, lambda *_: out, slab, panels, pivots)


def solution(mesh):
    in_specs = (P("prow", "pcol"), P(None, "prow", "pcol"), P())
    out_specs = P("prow", "pcol")
    return jax.shard_map(local, mesh=mesh, in_specs=in_specs, out_specs=out_specs, check_vma=False)
```
